32 devices in a mesh: slab: 8 (over y, x, core), grp: 4 (over z).
Axes of the slice: x: 2, y: 2, z: 4, core: 2. Of those that a mesh axis runs over, the one named last changes fastest.
Arguments:
- resid7: float32 [512, 4096], P(None, ('slab', 'grp')), may hold values from -6 to 6
- interp73: float32 [8, 4], replicated, may hold values from -2 to 2
- interp31: float32 [4, 2], replicated, may hold values from -4 to 4
- elem_ops: float32 [8, 8, 4096], P(None, None, 'slab'), as said below
- conn: int32 [8, 4096], P(None, 'slab'), may hold values from 0 to 1121, as said below
- faces: int32 [2, 8, 561], P(None, 'slab'), may hold values from 0 to 1121, as said below
Outputs:
- correction3: float32 [64, 4096], P(None, ('slab', 'grp'))
The draws below stay inside these ranges and needn't reach their ends.
Inputs may be any that keep to these rules, and one draw needn't show every extreme that they name: `conn`: the 512 columns of a slab describe a block of 32 x 16 x 1 hexahedra stacked along the long direction; column e lists the corners of one element, the corner at offsets (i, j, k) along (long, second, first direction) in row 4 i + 2 j + k; the slab's nodes are numbered 0 to 1121 in some order and every one of them is a corner of some element. faces[0, s] lists the 561 nodes of slab s on its face toward slab s - 1, faces[1, s] those on its face toward slab s + 1, all distinct; faces[1, s, f] and faces[0, s + 1, f] are the same point of the mesh. `elem_ops`: each element's matrix is symmetric, and each diagonal entry is positive and larger than the sum of magnitudes of the other entries of its row.
All inputs are finite; a program needn't handle non-finite values.
Results may differ from the reference program's by a relative error of at most 0.0003.
Values sent between devices are 32-bit elements; how exact they have to be, the bound alone decides.
A program may use at most 64 MiB of HBM per device.

```python
import math
import jax
import jax.numpy as jnp
from jax import lax

EX = 32
EY = 16
SWEEPS = 2
EG = 512
EZ = 1
NG = 1122
FACE = 561
ELEMS = 4096
N_SLAB = 8


def pin_ends(perm):
    top_at = jnp.argmax(perm == NG - 1)
    first = perm[0]
    perm = perm.at[top_at].set(first).at[0].set(NG - 1)
    target = EZ * FACE
    low_at = jnp.argmax(perm == 0)
    moved = perm[target]
    perm = perm.at[low_at].set(moved).at[target].set(0)
    return perm.astype(jnp.int32)


def slab_layout(key):
    base = jax.random.fold_in(key, 11)
    node_keys = jax.random.split(jax.random.fold_in(base, 1), N_SLAB)
    elem_keys = jax.random.split(jax.random.fold_in(base, 2), N_SLAB)
    node_perm = jax.vmap(lambda one: pin_ends(jax.random.permutation(one, NG).astype(jnp.int32)))(node_keys)
    elem_perm = jax.vmap(lambda one: jax.random.permutation(one, EG))(elem_keys).astype(jnp.int32)
    along_x = elem_perm % EX
    along_y = elem_perm // EX % EY
    along_z = elem_perm // (EX * EY)
    corner = jnp.arange(8, dtype=jnp.int32)
    off_z = (corner // 4)[None, :, None]
    off_y = (corner // 2 % 2)[None, :, None]
    off_x = (corner % 2)[None, :, None]
    lexical = ((along_z[:, None, :] + off_z) * (EY + 1) + along_y[:, None, :] + off_y) * (EX + 1) + along_x[:, None, :] + off_x
    corners = jax.vmap(lambda perm, where: perm[where])(node_perm, lexical)
    plane = jnp.arange(FACE, dtype=jnp.int32)
    lower = node_perm[:, plane]
    upper = node_perm[:, plane + EZ * FACE]
    return (corners.transpose(1, 0, 2).reshape(8, N_SLAB * EG), jnp.stack([lower, upper]))


def draw_conn(key, part):
    return slab_layout(key)[0]


def draw_faces(key, part):
    return slab_layout(key)[1]


def draw_elem_ops(key, part):
    first, second, third = jax.random.split(jax.random.fold_in(key, 5), 3)
    low_scale = 0.02
    raw = jax.random.uniform(first, (8, 8, ELEMS), jnp.float32, minval=-0.5, maxval=0.5)
    sym = 0.5 * (raw + jnp.swapaxes(raw, 0, 1))
    identity = jnp.eye(8, dtype=jnp.float32)[:, :, None]
    diagonal = 4.0 + jax.random.uniform(second, (8, ELEMS), jnp.float32)
    scale = jnp.exp(jax.random.uniform(third, (ELEMS,), jnp.float32, minval=math.log(low_scale), maxval=math.log(0.2)))
    return scale[None, None, :] * (sym * (1.0 - identity) + identity * diagonal[:, None, :])


def shard_levels(stream_key, extent, cuts, smallest, top_value):
    factor_of, own = 1.0, jax.random.fold_in(stream_key, 6)
    for dim, parts in cuts:
        draws = jnp.exp(jax.random.uniform(jax.random.fold_in(own, dim), (parts,), jnp.float32, smallest / len(cuts), top_value / len(cuts)))
        factor_of = factor_of * jnp.repeat(draws, extent[dim] // parts).reshape([-1 if axis == dim else 1 for axis in range(len(extent))])
    return factor_of


def normal_values(key, extent, deviation, most, cuts=(), kind=jnp.bfloat16):
    values = jax.random.normal(key, extent, jnp.float32) * deviation
    if len(cuts) > 0:
        values = shard_levels(key, extent, cuts, -0.22, 0.18) * values
    return jnp.clip(values, min=-most, max=most).astype(kind)


def setup_inputs(seed: int = 0) -> dict:
    key_of = jax.random.split(jax.random.key(seed), 7)
    return {
        "resid7": normal_values(key_of[0], (512, ELEMS), 1.0, 6.0, ((1, 32),), jnp.float32),
        "interp73": normal_values(key_of[1], (8, 4), 8 ** -0.5, 2.0, (), jnp.float32),
        "interp31": normal_values(key_of[2], (4, 2), 2 ** -0.5, 4.0, (), jnp.float32),
        "elem_ops": draw_elem_ops(jax.random.fold_in(key_of[6], 71), 0),
        "conn": draw_conn(jax.random.fold_in(key_of[6], 71), 0),
        "faces": draw_faces(jax.random.fold_in(key_of[6], 71), 0),
    }


lam_low = 0.3
lam_high = 1.9


def restrict(block, interp73, interp31):
    hi = lax.Precision.HIGHEST
    width = block.shape[1]
    cube = block.reshape(8, 8, 8, width)
    cube = jnp.einsum("kc,ijkm->ijcm", interp73, cube, precision=hi)
    cube = jnp.einsum("jb,ijcm->ibcm", interp73, cube, precision=hi)
    cube = jnp.einsum("ia,ibcm->abcm", interp73, cube, precision=hi)
    cube = jnp.einsum("kc,ijkm->ijcm", interp31, cube, precision=hi)
    cube = jnp.einsum("jb,ijcm->ibcm", interp31, cube, precision=hi)
    cube = jnp.einsum("ia,ibcm->abcm", interp31, cube, precision=hi)
    return cube.reshape(8, width)


def prolong(coarse, interp31):
    hi = lax.Precision.HIGHEST
    width = coarse.shape[1]
    cube = coarse.reshape(2, 2, 2, width)
    cube = jnp.einsum("ck,ijkm->ijcm", interp31, cube, precision=hi)
    cube = jnp.einsum("bj,ijcm->ibcm", interp31, cube, precision=hi)
    cube = jnp.einsum("ai,ibcm->abcm", interp31, cube, precision=hi)
    return cube.reshape(64, width)


def reference(resid7, interp73, interp31, elem_ops, conn, faces):
    hi = lax.Precision.HIGHEST

    def reduce_slab(index):
        block = lax.dynamic_slice_in_dim(resid7, index * EG, EG, 1)
        return restrict(block, interp73, interp31)

    coarse_res = lax.map(reduce_slab, jnp.arange(N_SLAB, dtype=jnp.int32))
    conn_slab = conn.reshape(8, N_SLAB, EG).transpose(1, 0, 2)
    ops_slab = elem_ops.reshape(8, 8, N_SLAB, EG).transpose(2, 0, 1, 3)
    lower = faces[0]
    upper = faces[1]

    def assemble(values):
        return jax.vmap(lambda vals, ids: jax.ops.segment_sum(vals.reshape(-1), ids.reshape(-1), num_segments=NG))(values, conn_slab)

    def share(nodes):
        bottom = jnp.take_along_axis(nodes, lower, 1)
        top = jnp.take_along_axis(nodes, upper, 1)
        zero_row = jnp.zeros((1, FACE), jnp.float32)
        below = jnp.concatenate([zero_row, top[:-1]], axis=0)
        above = jnp.concatenate([bottom[1:], zero_row], axis=0)
        return jax.vmap(lambda node, low, upp, bel, abo: node.at[low].add(bel).at[upp].add(abo))(nodes, lower, upper, below, above)

    def pick(field):
        return jax.vmap(lambda values, ids: values[ids])(field, conn_slab)

    def operate(field):
        local = jnp.einsum("spqe,sqe->spe", ops_slab, pick(field), precision=hi)
        return share(assemble(local))

    rhs = share(assemble(coarse_res))
    diag = share(assemble(jnp.einsum("sppe->spe", ops_slab)))
    theta = 0.5 * (lam_high + lam_low)
    delta = 0.5 * (lam_high - lam_low)
    sigma = theta / delta
    inverse = 1.0 / diag
    direction = inverse * rhs / theta
    solution = direction
    remain = rhs
    rho = 1.0 / sigma
    for sweep in range(SWEEPS):
        remain = remain - operate(direction)
        rho_new = 1.0 / (2.0 * sigma - rho)
        direction = (rho_new * rho) * direction + (2.0 * rho_new / delta) * inverse * remain
        solution = solution + direction
        rho = rho_new
    picked = pick(solution).transpose(1, 0, 2).reshape(8, ELEMS)
    return prolong(picked, interp31)
```

```python
import functools

import jax
import jax.numpy as jnp
from jax import lax
from jax.experimental import pallas as pl
from jax.experimental.pallas import tpu as pltpu
from jax.sharding import PartitionSpec as P

EX = 32
EY = 16
SWEEPS = 2


lam_low = 0.3
lam_high = 1.9


def extended(array, sides, width):
    for axis, dim in sides:
        count, length = (lax.axis_size(axis), array.shape[dim])
        up = [(i, (i + 1) % count) for i in range(count - 1)]
        down = [(j, i) for i, j in up]
        last = lax.slice_in_dim(array, length - width, length, axis=dim)
        first = lax.slice_in_dim(array, 0, width, axis=dim)
        before = lax.ppermute(last, axis, up)
        after = lax.ppermute(first, axis, down)
        array = jnp.concatenate([before, array, after], axis=dim)
    return array


def restrict_high(block, interp73):
    hi = lax.Precision.HIGHEST
    width = block.shape[1]
    cube = block.reshape(8, 8, 8, width)
    cube = jnp.einsum("kc,ijkm->ijcm", interp73, cube, precision=hi)
    cube = jnp.einsum("jb,ijcm->ibcm", interp73, cube, precision=hi)
    cube = jnp.einsum("ia,ibcm->abcm", interp73, cube, precision=hi)
    return cube.reshape(64, width)


def restrict_low(block, interp31):
    hi = lax.Precision.HIGHEST
    width = block.shape[1]
    cube = block.reshape(4, 4, 4, width)
    cube = jnp.einsum("kc,ijkm->ijcm", interp31, cube, precision=hi)
    cube = jnp.einsum("jb,ijcm->ibcm", interp31, cube, precision=hi)
    cube = jnp.einsum("ia,ibcm->abcm", interp31, cube, precision=hi)
    return cube.reshape(8, width)


def prolong(coarse, interp31):
    hi = lax.Precision.HIGHEST
    width = coarse.shape[1]
    cube = coarse.reshape(2, 2, 2, width)
    cube = jnp.einsum("ck,ijkm->ijcm", interp31, cube, precision=hi)
    cube = jnp.einsum("bj,ijcm->ibcm", interp31, cube, precision=hi)
    cube = jnp.einsum("ai,ibcm->abcm", interp31, cube, precision=hi)
    return cube.reshape(64, width)


def assemble(values, conn_ids, count):
    layers = values.shape[0]
    flat = values.reshape(layers, -1).T
    summed = jax.ops.segment_sum(flat, conn_ids.reshape(-1), num_segments=count)
    return summed.T


def element_term(operators, conn_ids, field):
    return jnp.einsum("pqe,qe->pe", operators, field[conn_ids], precision=lax.Precision.HIGHEST)


def share(nodes, faces):
    lower = faces[0, 0]
    upper = faces[1, 0]
    planes = jnp.stack([nodes[:, lower], nodes[:, upper]], axis=1)
    padded = extended(planes, (("slab", 1),), 1)
    return nodes.at[:, lower].add(padded[:, 0]).at[:, upper].add(padded[:, 3])


def local(resid7, interp73, interp31, elem_ops, conn, faces):
    own = resid7.shape[1]
    slab_elems = conn.shape[1]
    layers = slab_elems // (EX * EY)
    count = (EX + 1) * (EY + 1) * (layers + 1)
    start = lax.axis_index("grp") * own
    own_conn = lax.dynamic_slice_in_dim(conn, start, own, 1)
    middle_res = restrict_high(resid7, interp73)
    blocks = lax.all_gather(middle_res, "grp", axis=1, tiled=True)
    slab_res = restrict_low(blocks, interp31)
    pair = jnp.stack([slab_res, jnp.einsum("ppe->pe", elem_ops)])
    both_nodes = assemble(pair, conn, count)
    shared = share(both_nodes, faces)
    rhs = shared[0]
    diag = shared[1]
    theta = 0.5 * (lam_high + lam_low)
    delta = 0.5 * (lam_high - lam_low)
    sigma = theta / delta
    inverse = 1.0 / diag
    direction = inverse * rhs / theta
    solution = direction
    remain = rhs
    rho = 1.0 / sigma
    for sweep in range(SWEEPS):
        nodes = assemble(element_term(elem_ops, conn, direction)[None], conn, count)
        remain = remain - share(nodes, faces)[0]
        rho_new = 1.0 / (2.0 * sigma - rho)
        direction = rho_new * rho * direction + 2.0 * rho_new / delta * inverse * remain
        solution = solution + direction
        rho = rho_new
    return prolong(solution[own_conn], interp31)


STRIDE = EX + 1
POINTS = (EX + 1) * (EY + 1)
LANES = (POINTS + 127) // 128 * 128
LINE = EX * EY
BLOCKS = LINE // 128
MESH = pl.DeviceIdType.MESH
VMEM = pl.BlockSpec(memory_space=pltpu.VMEM)
SMEM = pl.BlockSpec(memory_space=pltpu.SMEM)


def rows_of(shape):
    return lax.broadcasted_iota(jnp.int32, shape, 0)


def spread(row, count=8):
    return jnp.broadcast_to(row, (count, row.shape[1]))


def stack_rows(rows):
    sub = rows_of((8, rows[0].shape[1]))
    out = spread(rows[0])
    for at in range(1, 8):
        out = jnp.where(sub == at, spread(rows[at]), out)
    return out


def parts_of(value):
    hi = value.astype(jnp.bfloat16).astype(jnp.float32)
    left = value - hi
    mid = left.astype(jnp.bfloat16).astype(jnp.float32)
    return jnp.concatenate([hi, mid, left - mid], axis=0).astype(jnp.bfloat16)


def join_parts(value):
    third = value.shape[0] // 3
    return value[:third] + value[third : 2 * third] + value[2 * third :]


def gather_sums(corners):
    sub = rows_of(corners.shape)
    odd, second = (sub % 2 == 1, sub // 2 % 2 == 1)
    part = jnp.where(odd, pltpu.roll(corners, 1, 1), corners)
    part = part + jnp.where(odd, pltpu.roll(part, 1, 0), pltpu.roll(part, 7, 0))
    part = jnp.where(second, pltpu.roll(part, STRIDE, 1), part)
    return part + jnp.where(second, pltpu.roll(part, 2, 0), pltpu.roll(part, 6, 0))


def corner_values(nodes):
    sub = rows_of(nodes.shape)
    part = jnp.where(sub // 2 % 2 == 1, pltpu.roll(nodes, LANES - STRIDE, 1), nodes)
    return jnp.where(sub % 2 == 1, pltpu.roll(part, LANES - 1, 1), part)


def before(ids, mine, theirs):
    column = jnp.broadcast_to(ids[theirs : theirs + 1], (128, LINE)).T
    row = spread(ids[mine : mine + 1])
    place = rows_of((8, LINE)).astype(jnp.float32)
    total = jnp.zeros((8, LINE), jnp.float32)
    for at in range(LINE // 8):
        one = column[8 * at : 8 * at + 8]
        same = jnp.concatenate([one] * BLOCKS, axis=1) == row
        total = total + jnp.where(same, place + (8.0 * at + 1.0), 0.0)
    return jnp.sum(total, axis=0, keepdims=True)


def positions(conn):
    ids = conn.astype(jnp.float32)
    own = lax.broadcasted_iota(jnp.int32, (1, LINE), 1)
    rows = []
    for theirs in (1, 2):
        found = before(ids, 0, theirs).astype(jnp.int32)
        packed = jnp.where(found > 0, found - 1 + LINE, own)
        rows += [packed[:, 128 * b : 128 * b + 128] for b in range(BLOCKS)]
    state = stack_rows(rows)
    sub = rows_of((8, 128))
    for _ in range((EX - 1).bit_length()):
        target = state % LINE
        lane, block = (target % 128, target // 128)
        got = jnp.zeros((8, 128), jnp.int32)
        for b in range(BLOCKS):
            table = jnp.where(sub < BLOCKS, spread(state[b : b + 1]), spread(state[BLOCKS + b : BLOCKS + b + 1]))
            got = jnp.where(block == b, jnp.take_along_axis(table, lane, axis=1), got)
        state = got + (state - target)
    steps = state // LINE
    return steps + STRIDE * pltpu.roll(steps, 4, 0)


def one_hot(row):
    return jnp.where(rows_of((LANES, row.shape[1])) == spread(row, LANES), 1.0, 0.0).astype(jnp.bfloat16)


def setup_kernel(conn_ref, ops_ref, res_ref, table_ref, i73_ref, i31_ref, lex_ref, send_ref, pos_ref):
    group = lax.axis_index("grp")
    coef = [[sum(i73_ref[i, m] * i31_ref[m, a] for m in range(4)) for a in range(2)] for i in range(8)]
    place = positions(conn_ref[...])

    along_j = [[None] * 8, [None] * 8]
    for j in range(8):
        for a in range(2):
            along_j[a][j] = sum(coef[i][a] * res_ref[64 * i + 8 * j : 64 * i + 8 * j + 8, :] for i in range(8))
    last = [sum(table_ref[:, m : m + 1] * i31_ref[m, c] for m in range(4)) for c in range(2)]
    rows = []
    for a in range(2):
        for b in range(2):
            line = sum(coef[j][b] * along_j[a][j] for j in range(8))
            for c in range(2):
                rows.append(jnp.sum(last[c] * line, axis=0, keepdims=True))
    low_res = stack_rows(rows)
    lanes = pl.ds(pl.multiple_of(group * 128, 128), 128)
    diagonal = stack_rows([ops_ref[p, p : p + 1, lanes] for p in range(8)])

    mine = spread(place[0:1])
    for b in range(1, BLOCKS):
        mine = jnp.where(group == b, spread(place[b : b + 1]), mine)
    pos_ref[...] = mine[0:1]
    own_hot = one_hot(mine[0:1])
    both = parts_of(jnp.concatenate([low_res, diagonal], axis=0))
    both = join_parts(lax.dot_general(both, own_hot, (((1,), (1,)), ((), ())), preferred_element_type=jnp.float32))
    for at in range(2):
        nodes = gather_sums(both[8 * at : 8 * at + 8])
        for plane in range(2):
            send_ref[plane, at : at + 1, :] = nodes[4 * plane : 4 * plane + 1]

    hot = jnp.concatenate([one_hot(place[b : b + 1]) for b in range(BLOCKS)], axis=1)
    ops = parts_of(ops_ref[...].reshape(64, LINE))
    lex = lax.dot_general(ops, hot, (((1,), (1,)), ((), ())), preferred_element_type=jnp.float32)
    lex_ref[...] = join_parts(lex).reshape(8, 8, LANES)


def smooth_kernel(slabs, groups, send_ref, lex_ref, pos_ref, table_ref, i31_ref, out_ref, got_own, got_side, out_side, in_side, own_send, own_recv, side_send, side_recv, face_send, face_recv):
    slab, group = (lax.axis_index("slab"), lax.axis_index("grp"))
    down, up = (lax.rem(slab + slabs - 1, slabs), lax.rem(slab + 1, slabs))
    has = (slab > 0, slab < slabs - 1)
    to = (down, up)

    barrier = pltpu.get_barrier_semaphore()
    peers = [lax.rem(group + k, groups) for k in range(groups)]
    for peer in peers[1:]:
        pl.semaphore_signal(barrier, inc=1, device_id=(slab, peer), device_id_type=MESH)
    for side in range(2):

        @pl.when(has[side])
        def _():
            for peer in peers:
                pl.semaphore_signal(barrier, inc=1, device_id=(to[side], peer), device_id_type=MESH)

    for side in range(2):

        @pl.when(jnp.logical_not(has[side]))
        def _():
            got_side[side] = jnp.zeros(got_side.shape[1:], jnp.float32)
            for sweep in range(SWEEPS):
                in_side[sweep, side] = jnp.zeros(in_side.shape[2:], jnp.float32)

    sides = has[0].astype(jnp.int32) + has[1].astype(jnp.int32)
    pl.semaphore_wait(barrier, groups - 1 + groups * sides)

    side_copies = [
        [
            pltpu.make_async_remote_copy(
                src_ref=send_ref.at[side],
                dst_ref=got_side.at[1 - side, k],
                send_sem=side_send.at[side, k],
                recv_sem=side_recv.at[1 - side, k],
                device_id=(to[side], peers[k]),
                device_id_type=MESH,
            )
            for k in range(groups)
        ]
        for side in range(2)
    ]
    own_copies = [
        pltpu.make_async_remote_copy(
            src_ref=send_ref,
            dst_ref=got_own.at[k - 1],
            send_sem=own_send.at[k - 1],
            recv_sem=own_recv.at[k - 1],
            device_id=(slab, peers[k]),
            device_id_type=MESH,
        )
        for k in range(1, groups)
    ]
    for side in range(2):

        @pl.when(has[side])
        def _():
            for copy in side_copies[side]:
                copy.start()

    for copy in own_copies:
        copy.start()

    sub = rows_of((8, LANES))
    own_hot = one_hot(pos_ref[...])

    def planes(low, high):
        return jnp.where(sub < 4, spread(low), spread(high))

    for copy in own_copies:
        copy.wait_recv()
    for side in range(2):

        @pl.when(has[side])
        def _():
            for copy in side_copies[1 - side]:
                copy.wait_recv()

    sums = []
    for plane in range(2):
        total = send_ref[plane]
        for k in range(groups - 1):
            total = total + got_own[k, plane]
        extra = got_side[plane, 0]
        for k in range(1, groups):
            extra = extra + got_side[plane, k]
        sums.append(total + extra)
    rhs = planes(sums[0][0:1], sums[1][0:1])
    diag = planes(sums[0][1:2], sums[1][1:2])
    real = lax.broadcasted_iota(jnp.int32, (8, LANES), 1) < POINTS
    inverse = 1.0 / jnp.where(real, diag, 1.0)

    theta = 0.5 * (lam_high + lam_low)
    delta = 0.5 * (lam_high - lam_low)
    sigma = theta / delta
    direction = inverse * rhs * (1.0 / theta)
    answer = direction
    remain = rhs
    rho = 1.0 / sigma
    faces = []
    for sweep in range(SWEEPS):
        corners = corner_values(direction)
        product = lex_ref[0] * spread(corners[0:1])
        for q in range(1, 8):
            product = product + lex_ref[q] * spread(corners[q : q + 1])
        nodes = gather_sums(product)
        for side in range(2):
            out_side[sweep, side] = nodes[4 * side : 4 * side + 1]
        pair = [
            pltpu.make_async_remote_copy(
                src_ref=out_side.at[sweep, side],
                dst_ref=in_side.at[sweep, 1 - side],
                send_sem=face_send.at[sweep, side],
                recv_sem=face_recv.at[sweep, 1 - side],
                device_id=(to[side], group),
                device_id_type=MESH,
            )
            for side in range(2)
        ]
        faces.append(pair)
        for side in range(2):

            @pl.when(has[side])
            def _():
                pair[side].start()

        for side in range(2):

            @pl.when(has[side])
            def _():
                pair[1 - side].wait_recv()

        remain = remain - (nodes + planes(in_side[sweep, 0], in_side[sweep, 1]))
        rho_new = 1.0 / (2.0 * sigma - rho)
        direction = rho_new * rho * direction + 2.0 * rho_new / delta * inverse * remain
        answer = answer + direction
        rho = rho_new

    picked = join_parts(jnp.dot(parts_of(corner_values(answer)), own_hot, preferred_element_type=jnp.float32))
    fine = jnp.concatenate([table_ref[...], table_ref[...]], axis=0)
    half = rows_of((8, 1)) < 4
    for h in range(2):
        weights = [
            jnp.broadcast_to(jnp.where(half, i31_ref[2 * h, j], i31_ref[2 * h + 1, j]) * fine[:, k : k + 1], (8, 128))
            for j in range(2)
            for k in range(2)
        ]
        for a in range(4):
            value = i31_ref[a, 0] * picked[0:4] + i31_ref[a, 1] * picked[4:8]
            block = sum(weights[q] * spread(value[q : q + 1]) for q in range(4))
            out_ref[8 * (2 * a + h) : 8 * (2 * a + h) + 8, :] = block

    for copy in own_copies:
        copy.wait_send()
    for side in range(2):

        @pl.when(has[side])
        def _():
            for copy in side_copies[side]:
                copy.wait_send()
            for pair in faces:
                pair[side].wait_send()


def one_layer(resid7, interp73, interp31, elem_ops, conn):
    slabs, groups = (lax.axis_size("slab"), lax.axis_size("grp"))
    lex, send, place = pl.pallas_call(
        setup_kernel,
        out_shape=(
            jax.ShapeDtypeStruct((8, 8, LANES), jnp.float32),
            jax.ShapeDtypeStruct((2, 2, LANES), jnp.float32),
            jax.ShapeDtypeStruct((1, 128), jnp.int32),
        ),
        in_specs=[VMEM] * 4 + [SMEM] * 2,
        out_specs=(VMEM,) * 3,
    )(conn, elem_ops, resid7, interp73, interp73, interp31)
    dma = pltpu.SemaphoreType.DMA
    return pl.pallas_call(
        functools.partial(smooth_kernel, slabs, groups),
        out_shape=jax.ShapeDtypeStruct((64, 128), jnp.float32),
        in_specs=[VMEM] * 4 + [SMEM],
        out_specs=VMEM,
        scratch_shapes=[
            pltpu.VMEM((groups - 1, 2, 2, LANES), jnp.float32),
            pltpu.VMEM((2, groups, 2, LANES), jnp.float32),
            pltpu.VMEM((SWEEPS, 2, 1, LANES), jnp.float32),
            pltpu.VMEM((SWEEPS, 2, 1, LANES), jnp.float32),
            dma((groups - 1,)),
            dma((groups - 1,)),
            dma((2, groups)),
            dma((2, groups)),
            dma((SWEEPS, 2)),
            dma((SWEEPS, 2)),
        ],
        compiler_params=pltpu.CompilerParams(collective_id=0, has_side_effects=True),
    )(send, lex, place, interp31, interp31)


def dispatch(resid7, interp73, interp31, elem_ops, conn, faces):
    if conn.shape[1] == LINE and resid7.shape[1] == 128 and lax.axis_size("grp") > 1:
        return one_layer(resid7, interp73, interp31, elem_ops, conn)
    return local(resid7, interp73, interp31, elem_ops, conn, faces)


def solution(mesh):
    in_specs = (
        P(None, ("slab", "grp")),
        P(),
        P(),
        P(None, None, "slab"),
        P(None, "slab"),
        P(None, "slab", None),
    )
    out_specs = P(None, ("slab", "grp"))
    return jax.shard_map(dispatch, mesh=mesh, in_specs=in_specs, out_specs=out_specs, check_vma=False)
```

```python
import functools

import jax
import jax.numpy as jnp
from jax import lax
from jax.experimental import pallas as pl
from jax.experimental.pallas import tpu as pltpu
from jax.sharding import PartitionSpec as P

EX = 32
EY = 16
SWEEPS = 2


lam_low = 0.3
lam_high = 1.9


def extended(array, sides, width):
    for axis, dim in sides:
        count, length = (lax.axis_size(axis), array.shape[dim])
        up = [(i, (i + 1) % count) for i in range(count - 1)]
        down = [(j, i) for i, j in up]
        last = lax.slice_in_dim(array, length - width, length, axis=dim)
        first = lax.slice_in_dim(array, 0, width, axis=dim)
        before = lax.ppermute(last, axis, up)
        after = lax.ppermute(first, axis, down)
        array = jnp.concatenate([before, array, after], axis=dim)
    return array


def restrict_high(block, interp73):
    hi = lax.Precision.HIGHEST
    width = block.shape[1]
    cube = block.reshape(8, 8, 8, width)
    cube = jnp.einsum("kc,ijkm->ijcm", interp73, cube, precision=hi)
    cube = jnp.einsum("jb,ijcm->ibcm", interp73, cube, precision=hi)
    cube = jnp.einsum("ia,ibcm->abcm", interp73, cube, precision=hi)
    return cube.reshape(64, width)


def restrict_low(block, interp31):
    hi = lax.Precision.HIGHEST
    width = block.shape[1]
    cube = block.reshape(4, 4, 4, width)
    cube = jnp.einsum("kc,ijkm->ijcm", interp31, cube, precision=hi)
    cube = jnp.einsum("jb,ijcm->ibcm", interp31, cube, precision=hi)
    cube = jnp.einsum("ia,ibcm->abcm", interp31, cube, precision=hi)
    return cube.reshape(8, width)


def prolong(coarse, interp31):
    hi = lax.Precision.HIGHEST
    width = coarse.shape[1]
    cube = coarse.reshape(2, 2, 2, width)
    cube = jnp.einsum("ck,ijkm->ijcm", interp31, cube, precision=hi)
    cube = jnp.einsum("bj,ijcm->ibcm", interp31, cube, precision=hi)
    cube = jnp.einsum("ai,ibcm->abcm", interp31, cube, precision=hi)
    return cube.reshape(64, width)


def assemble(values, conn_ids, count):
    layers = values.shape[0]
    flat = values.reshape(layers, -1).T
    summed = jax.ops.segment_sum(flat, conn_ids.reshape(-1), num_segments=count)
    return summed.T


def element_term(operators, conn_ids, field):
    return jnp.einsum("pqe,qe->pe", operators, field[conn_ids], precision=lax.Precision.HIGHEST)


def share(nodes, faces):
    lower = faces[0, 0]
    upper = faces[1, 0]
    planes = jnp.stack([nodes[:, lower], nodes[:, upper]], axis=1)
    padded = extended(planes, (("slab", 1),), 1)
    return nodes.at[:, lower].add(padded[:, 0]).at[:, upper].add(padded[:, 3])


def local(resid7, interp73, interp31, elem_ops, conn, faces):
    own = resid7.shape[1]
    slab_elems = conn.shape[1]
    layers = slab_elems // (EX * EY)
    count = (EX + 1) * (EY + 1) * (layers + 1)
    start = lax.axis_index("grp") * own
    own_conn = lax.dynamic_slice_in_dim(conn, start, own, 1)
    middle_res = restrict_high(resid7, interp73)
    blocks = lax.all_gather(middle_res, "grp", axis=1, tiled=True)
    slab_res = restrict_low(blocks, interp31)
    pair = jnp.stack([slab_res, jnp.einsum("ppe->pe", elem_ops)])
    both_nodes = assemble(pair, conn, count)
    shared = share(both_nodes, faces)
    rhs = shared[0]
    diag = shared[1]
    theta = 0.5 * (lam_high + lam_low)
    delta = 0.5 * (lam_high - lam_low)
    sigma = theta / delta
    inverse = 1.0 / diag
    direction = inverse * rhs / theta
    solution = direction
    remain = rhs
    rho = 1.0 / sigma
    for sweep in range(SWEEPS):
        nodes = assemble(element_term(elem_ops, conn, direction)[None], conn, count)
        remain = remain - share(nodes, faces)[0]
        rho_new = 1.0 / (2.0 * sigma - rho)
        direction = rho_new * rho * direction + 2.0 * rho_new / delta * inverse * remain
        solution = solution + direction
        rho = rho_new
    return prolong(solution[own_conn], interp31)


STRIDE = EX + 1
POINTS = (EX + 1) * (EY + 1)
LANES = (POINTS + 127) // 128 * 128
LINE = EX * EY
BLOCKS = LINE // 128
MESH = pl.DeviceIdType.MESH
VMEM = pl.BlockSpec(memory_space=pltpu.VMEM)
SMEM = pl.BlockSpec(memory_space=pltpu.SMEM)


def rows_of(shape):
    return lax.broadcasted_iota(jnp.int32, shape, 0)


def spread(row, count=8):
    return jnp.broadcast_to(row, (count, row.shape[1]))


def stack_rows(rows):
    sub = rows_of((8, rows[0].shape[1]))
    out = spread(rows[0])
    for at in range(1, 8):
        out = jnp.where(sub == at, spread(rows[at]), out)
    return out


def parts_of(value):
    hi = value.astype(jnp.bfloat16).astype(jnp.float32)
    left = value - hi
    mid = left.astype(jnp.bfloat16).astype(jnp.float32)
    return jnp.concatenate([hi, mid, left - mid], axis=0).astype(jnp.bfloat16)


def join_parts(value):
    third = value.shape[0] // 3
    return value[:third] + value[third : 2 * third] + value[2 * third :]


def gather_sums(corners):
    sub = rows_of(corners.shape)
    odd, second = (sub % 2 == 1, sub // 2 % 2 == 1)
    part = jnp.where(odd, pltpu.roll(corners, 1, 1), corners)
    part = part + jnp.where(odd, pltpu.roll(part, 1, 0), pltpu.roll(part, 7, 0))
    part = jnp.where(second, pltpu.roll(part, STRIDE, 1), part)
    return part + jnp.where(second, pltpu.roll(part, 2, 0), pltpu.roll(part, 6, 0))


def corner_values(nodes):
    sub = rows_of(nodes.shape)
    part = jnp.where(sub // 2 % 2 == 1, pltpu.roll(nodes, LANES - STRIDE, 1), nodes)
    return jnp.where(sub % 2 == 1, pltpu.roll(part, LANES - 1, 1), part)


def before(ids, mine, theirs):
    column = jnp.broadcast_to(ids[theirs : theirs + 1], (128, LINE)).T
    row = spread(ids[mine : mine + 1])
    place = rows_of((8, LINE)).astype(jnp.float32)
    total = jnp.zeros((8, LINE), jnp.float32)
    for at in range(LINE // 8):
        one = column[8 * at : 8 * at + 8]
        same = jnp.concatenate([one] * BLOCKS, axis=1) == row
        total = total + jnp.where(same, place + (8.0 * at + 1.0), 0.0)
    return jnp.sum(total, axis=0, keepdims=True)


def positions(conn):
    ids = conn.astype(jnp.float32)
    own = lax.broadcasted_iota(jnp.int32, (1, LINE), 1)
    rows = []
    for theirs in (1, 2):
        found = before(ids, 0, theirs).astype(jnp.int32)
        packed = jnp.where(found > 0, found - 1 + LINE, own)
        rows += [packed[:, 128 * b : 128 * b + 128] for b in range(BLOCKS)]
    state = stack_rows(rows)
    sub = rows_of((8, 128))
    for _ in range((EX - 1).bit_length()):
        target = state % LINE
        lane, block = (target % 128, target // 128)
        got = jnp.zeros((8, 128), jnp.int32)
        for b in range(BLOCKS):
            table = jnp.where(sub < BLOCKS, spread(state[b : b + 1]), spread(state[BLOCKS + b : BLOCKS + b + 1]))
            got = jnp.where(block == b, jnp.take_along_axis(table, lane, axis=1), got)
        state = got + (state - target)
    steps = state // LINE
    return steps + STRIDE * pltpu.roll(steps, 4, 0)


def one_hot(row):
    return jnp.where(rows_of((LANES, row.shape[1])) == spread(row, LANES), 1.0, 0.0).astype(jnp.bfloat16)


def cycle_kernel(slabs, groups, conn_ref, ops_ref, res_ref, i73_ref, i31_ref, out_ref, lex_ref, send_ref, got_own, got_side, out_side, in_side, own_send, own_recv, side_send, side_recv, face_send, face_recv):
    slab, group = (lax.axis_index("slab"), lax.axis_index("grp"))
    down, up = (lax.rem(slab + slabs - 1, slabs), lax.rem(slab + 1, slabs))
    has = (slab > 0, slab < slabs - 1)
    to = (down, up)

    barrier = pltpu.get_barrier_semaphore()
    peers = [lax.rem(group + k, groups) for k in range(groups)]
    for peer in peers[1:]:
        pl.semaphore_signal(barrier, inc=1, device_id=(slab, peer), device_id_type=MESH)
    for side in range(2):

        @pl.when(has[side])
        def _():
            for peer in peers:
                pl.semaphore_signal(barrier, inc=1, device_id=(to[side], peer), device_id_type=MESH)

    for side in range(2):

        @pl.when(jnp.logical_not(has[side]))
        def _():
            got_side[side] = jnp.zeros(got_side.shape[1:], jnp.float32)
            for sweep in range(SWEEPS):
                in_side[sweep, side] = jnp.zeros(in_side.shape[2:], jnp.float32)

    coef = [[sum(i73_ref[m, i] * i31_ref[a, m] for m in range(4)) for a in range(2)] for i in range(8)]
    along_j = [[None] * 8, [None] * 8]
    for j in range(8):
        for a in range(2):
            along_j[a][j] = sum(coef[i][a] * res_ref[64 * i + 8 * j : 64 * i + 8 * j + 8, :] for i in range(8))
    sub_tile = rows_of((8, 128))
    last = []
    for c in range(2):
        column = jnp.full((8, 128), coef[0][c], jnp.float32)
        for k in range(1, 8):
            column = jnp.where(sub_tile == k, coef[k][c], column)
        last.append(column)
    rows = []
    for a in range(2):
        for b in range(2):
            line = sum(coef[j][b] * along_j[a][j] for j in range(8))
            for c in range(2):
                rows.append(jnp.sum(last[c] * line, axis=0, keepdims=True))
    low_res = stack_rows(rows)
    lanes = pl.ds(pl.multiple_of(group * 128, 128), 128)
    diagonal = stack_rows([ops_ref[p, p : p + 1, lanes] for p in range(8)])

    place = positions(conn_ref[...])
    mine = spread(place[0:1])
    for b in range(1, BLOCKS):
        mine = jnp.where(group == b, spread(place[b : b + 1]), mine)
    own_hot = one_hot(mine[0:1])
    both = parts_of(jnp.concatenate([low_res, diagonal], axis=0))
    both = join_parts(lax.dot_general(both, own_hot, (((1,), (1,)), ((), ())), preferred_element_type=jnp.float32))
    for at in range(2):
        nodes = gather_sums(both[8 * at : 8 * at + 8])
        for plane in range(2):
            send_ref[plane, at : at + 1, :] = nodes[4 * plane : 4 * plane + 1]

    sides = has[0].astype(jnp.int32) + has[1].astype(jnp.int32)
    pl.semaphore_wait(barrier, groups - 1 + groups * sides)

    side_copies = [
        [
            pltpu.make_async_remote_copy(
                src_ref=send_ref.at[side],
                dst_ref=got_side.at[1 - side, k],
                send_sem=side_send.at[side, k],
                recv_sem=side_recv.at[1 - side, k],
                device_id=(to[side], peers[k]),
                device_id_type=MESH,
            )
            for k in range(groups)
        ]
        for side in range(2)
    ]
    own_copies = [
        pltpu.make_async_remote_copy(
            src_ref=send_ref,
            dst_ref=got_own.at[k - 1],
            send_sem=own_send.at[k - 1],
            recv_sem=own_recv.at[k - 1],
            device_id=(slab, peers[k]),
            device_id_type=MESH,
        )
        for k in range(1, groups)
    ]
    for side in range(2):

        @pl.when(has[side])
        def _():
            for copy in side_copies[side]:
                copy.start()

    for copy in own_copies:
        copy.start()

    sub = rows_of((8, LANES))
    hot = jnp.concatenate([one_hot(place[b : b + 1]) for b in range(BLOCKS)], axis=1)
    ops = parts_of(ops_ref[...].reshape(64, LINE))
    lex = lax.dot_general(ops, hot, (((1,), (1,)), ((), ())), preferred_element_type=jnp.float32)
    lex_ref[...] = join_parts(lex).reshape(8, 8, LANES)

    def planes(low, high):
        return jnp.where(sub < 4, spread(low), spread(high))

    for copy in own_copies:
        copy.wait_recv()
    for side in range(2):

        @pl.when(has[side])
        def _():
            for copy in side_copies[1 - side]:
                copy.wait_recv()

    sums = []
    for plane in range(2):
        total = send_ref[plane]
        for k in range(groups - 1):
            total = total + got_own[k, plane]
        extra = got_side[plane, 0]
        for k in range(1, groups):
            extra = extra + got_side[plane, k]
        sums.append(total + extra)
    rhs = planes(sums[0][0:1], sums[1][0:1])
    diag = planes(sums[0][1:2], sums[1][1:2])
    real = lax.broadcasted_iota(jnp.int32, (8, LANES), 1) < POINTS
    inverse = 1.0 / jnp.where(real, diag, 1.0)

    theta = 0.5 * (lam_high + lam_low)
    delta = 0.5 * (lam_high - lam_low)
    sigma = theta / delta
    direction = inverse * rhs * (1.0 / theta)
    answer = direction
    remain = rhs
    rho = 1.0 / sigma
    faces = []
    for sweep in range(SWEEPS):
        corners = corner_values(direction)
        product = lex_ref[0] * spread(corners[0:1])
        for q in range(1, 8):
            product = product + lex_ref[q] * spread(corners[q : q + 1])
        nodes = gather_sums(product)
        for side in range(2):
            out_side[sweep, side] = nodes[4 * side : 4 * side + 1]
        pair = [
            pltpu.make_async_remote_copy(
                src_ref=out_side.at[sweep, side],
                dst_ref=in_side.at[sweep, 1 - side],
                send_sem=face_send.at[sweep, side],
                recv_sem=face_recv.at[sweep, 1 - side],
                device_id=(to[side], group),
                device_id_type=MESH,
            )
            for side in range(2)
        ]
        faces.append(pair)
        for side in range(2):

            @pl.when(has[side])
            def _():
                pair[side].start()

        for side in range(2):

            @pl.when(has[side])
            def _():
                pair[1 - side].wait_recv()

        remain = remain - (nodes + planes(in_side[sweep, 0], in_side[sweep, 1]))
        rho_new = 1.0 / (2.0 * sigma - rho)
        direction = rho_new * rho * direction + 2.0 * rho_new / delta * inverse * remain
        answer = answer + direction
        rho = rho_new

    out_ref[...] = join_parts(jnp.dot(parts_of(corner_values(answer)), own_hot, preferred_element_type=jnp.float32))

    for copy in own_copies:
        copy.wait_send()
    for side in range(2):

        @pl.when(has[side])
        def _():
            for copy in side_copies[side]:
                copy.wait_send()
            for pair in faces:
                pair[side].wait_send()


def prolong_kernel(picked_ref, i31_ref, out_ref):
    picked = picked_ref[...]
    sub = rows_of((8, 128))
    fine = []
    for k in range(2):
        column = jnp.full((8, 128), i31_ref[k, 0], jnp.float32)
        for c in range(1, 4):
            column = jnp.where(sub % 4 == c, i31_ref[k, c], column)
        fine.append(column)
    for h in range(2):
        weights = [jnp.where(sub < 4, i31_ref[j, 2 * h], i31_ref[j, 2 * h + 1]) * fine[k] for j in range(2) for k in range(2)]
        for a in range(4):
            value = i31_ref[0, a] * picked[0:4] + i31_ref[1, a] * picked[4:8]
            block = sum(weights[q] * spread(value[q : q + 1]) for q in range(4))
            out_ref[8 * (2 * a + h) : 8 * (2 * a + h) + 8, :] = block


def one_layer(resid7, interp73, interp31, elem_ops, conn):
    slabs, groups = (lax.axis_size("slab"), lax.axis_size("grp"))
    dma = pltpu.SemaphoreType.DMA
    picked = pl.pallas_call(
        functools.partial(cycle_kernel, slabs, groups),
        out_shape=jax.ShapeDtypeStruct((8, 128), jnp.float32),
        in_specs=[VMEM] * 3 + [SMEM] * 2,
        out_specs=VMEM,
        scratch_shapes=[
            pltpu.VMEM((8, 8, LANES), jnp.float32),
            pltpu.VMEM((2, 2, LANES), jnp.float32),
            pltpu.VMEM((groups - 1, 2, 2, LANES), jnp.float32),
            pltpu.VMEM((2, groups, 2, LANES), jnp.float32),
            pltpu.VMEM((SWEEPS, 2, 1, LANES), jnp.float32),
            pltpu.VMEM((SWEEPS, 2, 1, LANES), jnp.float32),
            dma((groups - 1,)),
            dma((groups - 1,)),
            dma((2, groups)),
            dma((2, groups)),
            dma((SWEEPS, 2)),
            dma((SWEEPS, 2)),
        ],
        compiler_params=pltpu.CompilerParams(collective_id=0, has_side_effects=True),
    )(conn, elem_ops, resid7, interp73.T, interp31.T)
    return pl.pallas_call(
        prolong_kernel,
        out_shape=jax.ShapeDtypeStruct((64, 128), jnp.float32),
        in_specs=[VMEM, SMEM],
        out_specs=VMEM,
    )(picked, interp31.T)


def dispatch(resid7, interp73, interp31, elem_ops, conn, faces):
    if conn.shape[1] == LINE and resid7.shape[1] == 128 and lax.axis_size("grp") > 1:
        return one_layer(resid7, interp73, interp31, elem_ops, conn)
    return local(resid7, interp73, interp31, elem_ops, conn, faces)


def solution(mesh):
    in_specs = (
        P(None, ("slab", "grp")),
        P(),
        P(),
        P(None, None, "slab"),
        P(None, "slab"),
        P(None, "slab", None),
    )
    out_specs = P(None, ("slab", "grp"))
    return jax.shard_map(dispatch, mesh=mesh, in_specs=in_specs, out_specs=out_specs, check_vma=False)
```

```python
import functools

import jax
import jax.numpy as jnp
from jax import lax
from jax.experimental import pallas as pl
from jax.experimental.pallas import tpu as pltpu
from jax.sharding import PartitionSpec as P

EX = 32
EY = 16
SWEEPS = 2


lam_low = 0.3
lam_high = 1.9


def extended(array, sides, width):
    for axis, dim in sides:
        count, length = (lax.axis_size(axis), array.shape[dim])
        up = [(i, (i + 1) % count) for i in range(count - 1)]
        down = [(j, i) for i, j in up]
        last = lax.slice_in_dim(array, length - width, length, axis=dim)
        first = lax.slice_in_dim(array, 0, width, axis=dim)
        before = lax.ppermute(last, axis, up)
        after = lax.ppermute(first, axis, down)
        array = jnp.concatenate([before, array, after], axis=dim)
    return array


def restrict_high(block, interp73):
    hi = lax.Precision.HIGHEST
    width = block.shape[1]
    cube = block.reshape(8, 8, 8, width)
    cube = jnp.einsum("kc,ijkm->ijcm", interp73, cube, precision=hi)
    cube = jnp.einsum("jb,ijcm->ibcm", interp73, cube, precision=hi)
    cube = jnp.einsum("ia,ibcm->abcm", interp73, cube, precision=hi)
    return cube.reshape(64, width)


def restrict_low(block, interp31):
    hi = lax.Precision.HIGHEST
    width = block.shape[1]
    cube = block.reshape(4, 4, 4, width)
    cube = jnp.einsum("kc,ijkm->ijcm", interp31, cube, precision=hi)
    cube = jnp.einsum("jb,ijcm->ibcm", interp31, cube, precision=hi)
    cube = jnp.einsum("ia,ibcm->abcm", interp31, cube, precision=hi)
    return cube.reshape(8, width)


def prolong(coarse, interp31):
    hi = lax.Precision.HIGHEST
    width = coarse.shape[1]
    cube = coarse.reshape(2, 2, 2, width)
    cube = jnp.einsum("ck,ijkm->ijcm", interp31, cube, precision=hi)
    cube = jnp.einsum("bj,ijcm->ibcm", interp31, cube, precision=hi)
    cube = jnp.einsum("ai,ibcm->abcm", interp31, cube, precision=hi)
    return cube.reshape(64, width)


def assemble(values, conn_ids, count):
    layers = values.shape[0]
    flat = values.reshape(layers, -1).T
    summed = jax.ops.segment_sum(flat, conn_ids.reshape(-1), num_segments=count)
    return summed.T


def element_term(operators, conn_ids, field):
    return jnp.einsum("pqe,qe->pe", operators, field[conn_ids], precision=lax.Precision.HIGHEST)


def share(nodes, faces):
    lower = faces[0, 0]
    upper = faces[1, 0]
    planes = jnp.stack([nodes[:, lower], nodes[:, upper]], axis=1)
    padded = extended(planes, (("slab", 1),), 1)
    return nodes.at[:, lower].add(padded[:, 0]).at[:, upper].add(padded[:, 3])


def local(resid7, interp73, interp31, elem_ops, conn, faces):
    own = resid7.shape[1]
    slab_elems = conn.shape[1]
    layers = slab_elems // (EX * EY)
    count = (EX + 1) * (EY + 1) * (layers + 1)
    start = lax.axis_index("grp") * own
    own_conn = lax.dynamic_slice_in_dim(conn, start, own, 1)
    middle_res = restrict_high(resid7, interp73)
    blocks = lax.all_gather(middle_res, "grp", axis=1, tiled=True)
    slab_res = restrict_low(blocks, interp31)
    pair = jnp.stack([slab_res, jnp.einsum("ppe->pe", elem_ops)])
    both_nodes = assemble(pair, conn, count)
    shared = share(both_nodes, faces)
    rhs = shared[0]
    diag = shared[1]
    theta = 0.5 * (lam_high + lam_low)
    delta = 0.5 * (lam_high - lam_low)
    sigma = theta / delta
    inverse = 1.0 / diag
    direction = inverse * rhs / theta
    solution = direction
    remain = rhs
    rho = 1.0 / sigma
    for sweep in range(SWEEPS):
        nodes = assemble(element_term(elem_ops, conn, direction)[None], conn, count)
        remain = remain - share(nodes, faces)[0]
        rho_new = 1.0 / (2.0 * sigma - rho)
        direction = rho_new * rho * direction + 2.0 * rho_new / delta * inverse * remain
        solution = solution + direction
        rho = rho_new
    return prolong(solution[own_conn], interp31)


STRIDE = EX + 1
POINTS = (EX + 1) * (EY + 1)
LANES = (POINTS + 127) // 128 * 128
LINE = EX * EY
BLOCKS = LINE // 128
MESH = pl.DeviceIdType.MESH
VMEM = pl.BlockSpec(memory_space=pltpu.VMEM)
SMEM = pl.BlockSpec(memory_space=pltpu.SMEM)


def rows_of(shape):
    return lax.broadcasted_iota(jnp.int32, shape, 0)


def spread(row, count=8):
    return jnp.broadcast_to(row, (count, row.shape[1]))


def stack_rows(rows):
    sub = rows_of((8, rows[0].shape[1]))
    out = spread(rows[0])
    for at in range(1, 8):
        out = jnp.where(sub == at, spread(rows[at]), out)
    return out


def parts_of(value):
    hi = value.astype(jnp.bfloat16).astype(jnp.float32)
    left = value - hi
    mid = left.astype(jnp.bfloat16).astype(jnp.float32)
    return jnp.concatenate([hi, mid, left - mid], axis=0).astype(jnp.bfloat16)


def join_parts(value):
    third = value.shape[0] // 3
    return value[:third] + value[third : 2 * third] + value[2 * third :]


def gather_sums(corners):
    sub = rows_of(corners.shape)
    odd, second = (sub % 2 == 1, sub // 2 % 2 == 1)
    part = jnp.where(odd, pltpu.roll(corners, 1, 1), corners)
    part = part + jnp.where(odd, pltpu.roll(part, 1, 0), pltpu.roll(part, 7, 0))
    part = jnp.where(second, pltpu.roll(part, STRIDE, 1), part)
    return part + jnp.where(second, pltpu.roll(part, 2, 0), pltpu.roll(part, 6, 0))


def corner_values(nodes):
    sub = rows_of(nodes.shape)
    part = jnp.where(sub // 2 % 2 == 1, pltpu.roll(nodes, LANES - STRIDE, 1), nodes)
    return jnp.where(sub % 2 == 1, pltpu.roll(part, LANES - 1, 1), part)


def before(ids, mine, theirs):
    column = jnp.broadcast_to(ids[theirs : theirs + 1], (128, LINE)).T
    row = spread(ids[mine : mine + 1])
    place = rows_of((8, LINE)).astype(jnp.float32)
    total = jnp.zeros((8, LINE), jnp.float32)
    for at in range(LINE // 8):
        one = column[8 * at : 8 * at + 8]
        same = jnp.concatenate([one] * BLOCKS, axis=1) == row
        total = total + jnp.where(same, place + (8.0 * at + 1.0), 0.0)
    return jnp.sum(total, axis=0, keepdims=True)


def positions(conn):
    ids = conn.astype(jnp.float32)
    own = lax.broadcasted_iota(jnp.int32, (1, LINE), 1)
    rows = []
    for theirs in (1, 2):
        found = before(ids, 0, theirs).astype(jnp.int32)
        packed = jnp.where(found > 0, found - 1 + LINE, own)
        rows += [packed[:, 128 * b : 128 * b + 128] for b in range(BLOCKS)]
    state = stack_rows(rows)
    sub = rows_of((8, 128))
    for _ in range((EX - 1).bit_length()):
        target = state % LINE
        lane, block = (target % 128, target // 128)
        got = jnp.zeros((8, 128), jnp.int32)
        for b in range(BLOCKS):
            table = jnp.where(sub < BLOCKS, spread(state[b : b + 1]), spread(state[BLOCKS + b : BLOCKS + b + 1]))
            got = jnp.where(block == b, jnp.take_along_axis(table, lane, axis=1), got)
        state = got + (state - target)
    steps = state // LINE
    return steps + STRIDE * pltpu.roll(steps, 4, 0)


def one_hot(row):
    return jnp.where(rows_of((LANES, row.shape[1])) == spread(row, LANES), 1.0, 0.0).astype(jnp.bfloat16)


def cycle_kernel(slabs, groups, conn_ref, ops_ref, res_ref, i73_ref, i31_ref, out_ref, lex_ref, near_ref, send_ref, got_own, got_side, out_pack, in_pack, out_far, in_far, own_send, own_recv, side_send, side_recv, ops_send, ops_recv, pack_send, pack_recv, far_send, far_recv):
    slab, group = (lax.axis_index("slab"), lax.axis_index("grp"))
    down, up = (lax.rem(slab + slabs - 1, slabs), lax.rem(slab + 1, slabs))
    has = (slab > 0, slab < slabs - 1)
    to = (down, up)
    beyond = (slab > 1, slab < slabs - 2)
    skip = (lax.rem(slab + slabs - 2, slabs), lax.rem(slab + 2, slabs))

    barrier = pltpu.get_barrier_semaphore()
    peers = [lax.rem(group + k, groups) for k in range(groups)]
    for peer in peers[1:]:
        pl.semaphore_signal(barrier, inc=1, device_id=(slab, peer), device_id_type=MESH)
    for side in range(2):

        @pl.when(has[side])
        def _():
            for peer in peers:
                pl.semaphore_signal(barrier, inc=1, device_id=(to[side], peer), device_id_type=MESH)

        @pl.when(beyond[side])
        def _():
            pl.semaphore_signal(barrier, inc=1, device_id=(skip[side], group), device_id_type=MESH)

    for side in range(2):

        @pl.when(jnp.logical_not(has[side]))
        def _():
            got_side[side] = jnp.zeros(got_side.shape[1:], jnp.float32)
            in_pack[side] = jnp.where(rows_of((4, LANES)) == 3, 1.0, 0.0)
            near_ref[:, 4 * side : 4 * side + 4, :] = jnp.zeros((8, 4, LANES), jnp.float32)

        @pl.when(jnp.logical_not(beyond[side]))
        def _():
            in_far[side] = jnp.zeros((1, LANES), jnp.float32)

    coef = [[sum(i73_ref[m, i] * i31_ref[a, m] for m in range(4)) for a in range(2)] for i in range(8)]
    along_j = [[None] * 8, [None] * 8]
    for j in range(8):
        for a in range(2):
            along_j[a][j] = sum(coef[i][a] * res_ref[64 * i + 8 * j : 64 * i + 8 * j + 8, :] for i in range(8))
    sub_tile = rows_of((8, 128))
    last = []
    for c in range(2):
        column = jnp.full((8, 128), coef[0][c], jnp.float32)
        for k in range(1, 8):
            column = jnp.where(sub_tile == k, coef[k][c], column)
        last.append(column)
    rows = []
    for a in range(2):
        for b in range(2):
            line = sum(coef[j][b] * along_j[a][j] for j in range(8))
            for c in range(2):
                rows.append(jnp.sum(last[c] * line, axis=0, keepdims=True))
    low_res = stack_rows(rows)
    lanes = pl.ds(pl.multiple_of(group * 128, 128), 128)
    diagonal = stack_rows([ops_ref[p, p : p + 1, lanes] for p in range(8)])

    place = positions(conn_ref[...])
    mine = spread(place[0:1])
    for b in range(1, BLOCKS):
        mine = jnp.where(group == b, spread(place[b : b + 1]), mine)
    own_hot = one_hot(mine[0:1])
    both = parts_of(jnp.concatenate([low_res, diagonal], axis=0))
    both = join_parts(lax.dot_general(both, own_hot, (((1,), (1,)), ((), ())), preferred_element_type=jnp.float32))
    for at in range(2):
        nodes = gather_sums(both[8 * at : 8 * at + 8])
        for plane in range(2):
            send_ref[plane, at : at + 1, :] = nodes[4 * plane : 4 * plane + 1]

    sides = has[0].astype(jnp.int32) + has[1].astype(jnp.int32)
    far_sides = beyond[0].astype(jnp.int32) + beyond[1].astype(jnp.int32)
    pl.semaphore_wait(barrier, groups - 1 + groups * sides + far_sides)

    side_copies = [
        [
            pltpu.make_async_remote_copy(
                src_ref=send_ref.at[side],
                dst_ref=got_side.at[1 - side, k],
                send_sem=side_send.at[side, k],
                recv_sem=side_recv.at[1 - side, k],
                device_id=(to[side], peers[k]),
                device_id_type=MESH,
            )
            for k in range(groups)
        ]
        for side in range(2)
    ]
    own_copies = [
        pltpu.make_async_remote_copy(
            src_ref=send_ref,
            dst_ref=got_own.at[k - 1],
            send_sem=own_send.at[k - 1],
            recv_sem=own_recv.at[k - 1],
            device_id=(slab, peers[k]),
            device_id_type=MESH,
        )
        for k in range(1, groups)
    ]
    for side in range(2):

        @pl.when(has[side])
        def _():
            for copy in side_copies[side]:
                copy.start()

    for copy in own_copies:
        copy.start()

    sub = rows_of((8, LANES))
    hot = jnp.concatenate([one_hot(place[b : b + 1]) for b in range(BLOCKS)], axis=1)
    ops = parts_of(ops_ref[...].reshape(64, LINE))
    lex = lax.dot_general(ops, hot, (((1,), (1,)), ((), ())), preferred_element_type=jnp.float32)
    lex_ref[...] = join_parts(lex).reshape(8, 8, LANES)
    ops_copies = []
    for side in range(2):
        ops_copies.append(
            pltpu.make_async_remote_copy(
                src_ref=lex_ref.at[:, pl.ds(4 * side, 4), :],
                dst_ref=near_ref.at[:, pl.ds(4 - 4 * side, 4), :],
                send_sem=ops_send.at[side],
                recv_sem=ops_recv.at[1 - side],
                device_id=(to[side], group),
                device_id_type=MESH,
            )
        )

        @pl.when(has[side])
        def _():
            ops_copies[side].start()


    def planes(low, high):
        return jnp.where(sub < 4, spread(low), spread(high))

    for copy in own_copies:
        copy.wait_recv()
    for side in range(2):

        @pl.when(has[side])
        def _():
            for copy in side_copies[1 - side]:
                copy.wait_recv()

    sums = []
    for plane in range(2):
        total = send_ref[plane]
        for k in range(groups - 1):
            total = total + got_own[k, plane]
        extra = got_side[plane, 0]
        for k in range(1, groups):
            extra = extra + got_side[plane, k]
        sums.append(total + extra)
    rhs = planes(sums[0][0:1], sums[1][0:1])
    diag = planes(sums[0][1:2], sums[1][1:2])
    real = lax.broadcasted_iota(jnp.int32, (8, LANES), 1) < POINTS
    inverse = 1.0 / jnp.where(real, diag, 1.0)

    theta = 0.5 * (lam_high + lam_low)
    delta = 0.5 * (lam_high - lam_low)
    sigma = theta / delta
    first = inverse * rhs * (1.0 / theta)
    corners = corner_values(first)
    product = lex_ref[0] * spread(corners[0:1])
    for q in range(1, 8):
        product = product + lex_ref[q] * spread(corners[q : q + 1])
    nodes = gather_sums(product)
    pack_copies, far_copies = ([], [])
    for side in range(2):
        near, far = (4 * side, 4 - 4 * side)
        for at, value in enumerate((nodes[near : near + 1], nodes[far : far + 1], rhs[far : far + 1], diag[far : far + 1])):
            out_pack[side, at : at + 1, :] = value
        out_far[side] = nodes[near : near + 1]
        pack_copies.append(
            pltpu.make_async_remote_copy(
                src_ref=out_pack.at[side],
                dst_ref=in_pack.at[1 - side],
                send_sem=pack_send.at[side],
                recv_sem=pack_recv.at[1 - side],
                device_id=(to[side], group),
                device_id_type=MESH,
            )
        )
        far_copies.append(
            pltpu.make_async_remote_copy(
                src_ref=out_far.at[side],
                dst_ref=in_far.at[1 - side],
                send_sem=far_send.at[side],
                recv_sem=far_recv.at[1 - side],
                device_id=(skip[side], group),
                device_id_type=MESH,
            )
        )

        @pl.when(beyond[side])
        def _():
            far_copies[side].start()

        @pl.when(has[side])
        def _():
            pack_copies[side].start()

    for side in range(2):

        @pl.when(has[side])
        def _():
            ops_copies[1 - side].wait_recv()
            pack_copies[1 - side].wait_recv()

        @pl.when(beyond[side])
        def _():
            far_copies[1 - side].wait_recv()

    low, high = (in_pack[0], in_pack[1])
    far_inverse = 1.0 / jnp.where(real, planes(low[3:4], high[3:4]), 1.0)
    far_rhs = planes(low[2:3], high[2:3])
    far_first = far_inverse * far_rhs * (1.0 / theta)
    far_remain = far_rhs - planes(low[1:2] + in_far[0], high[1:2] + in_far[1])
    remain = rhs - (nodes + planes(low[0:1], high[0:1]))
    rho = 1.0 / sigma
    rho_new = 1.0 / (2.0 * sigma - rho)
    second = rho_new * rho * first + 2.0 * rho_new / delta * inverse * remain
    far_second = rho_new * rho * far_first + 2.0 * rho_new / delta * far_inverse * far_remain
    rho = rho_new
    rho_new = 1.0 / (2.0 * sigma - rho)

    corners = corner_values(second)
    ends = (jnp.where(sub < 4, far_second, second), jnp.where(sub < 4, second, far_second))
    product = lex_ref[0] * spread(corners[0:1])
    for q in range(1, 8):
        product = product + lex_ref[q] * spread(corners[q : q + 1])
    for q in range(8):
        shift = q // 2 % 2 * STRIDE + q % 2
        value = ends[q // 4]
        product = product + near_ref[q] * (pltpu.roll(value, LANES - shift, 1) if shift else value)
    remain = remain - gather_sums(product)
    third = rho_new * rho * second + 2.0 * rho_new / delta * inverse * remain
    answer = first + second + third

    out_ref[...] = join_parts(jnp.dot(parts_of(corner_values(answer)), own_hot, preferred_element_type=jnp.float32))

    for copy in own_copies:
        copy.wait_send()
    for side in range(2):

        @pl.when(has[side])
        def _():
            for copy in side_copies[side]:
                copy.wait_send()
            ops_copies[side].wait_send()
            pack_copies[side].wait_send()

        @pl.when(beyond[side])
        def _():
            far_copies[side].wait_send()


def prolong_kernel(picked_ref, i31_ref, out_ref):
    picked = picked_ref[...]
    sub = rows_of((8, 128))
    fine = []
    for k in range(2):
        column = jnp.full((8, 128), i31_ref[k, 0], jnp.float32)
        for c in range(1, 4):
            column = jnp.where(sub % 4 == c, i31_ref[k, c], column)
        fine.append(column)
    for h in range(2):
        weights = [jnp.where(sub < 4, i31_ref[j, 2 * h], i31_ref[j, 2 * h + 1]) * fine[k] for j in range(2) for k in range(2)]
        for a in range(4):
            value = i31_ref[0, a] * picked[0:4] + i31_ref[1, a] * picked[4:8]
            block = sum(weights[q] * spread(value[q : q + 1]) for q in range(4))
            out_ref[8 * (2 * a + h) : 8 * (2 * a + h) + 8, :] = block


def one_layer(resid7, interp73, interp31, elem_ops, conn):
    slabs, groups = (lax.axis_size("slab"), lax.axis_size("grp"))
    dma = pltpu.SemaphoreType.DMA
    picked = pl.pallas_call(
        functools.partial(cycle_kernel, slabs, groups),
        out_shape=pltpu.VMEM((8, 128), jnp.float32),
        in_specs=[VMEM] * 3 + [SMEM] * 2,
        out_specs=VMEM,
        scratch_shapes=[
            pltpu.VMEM((8, 8, LANES), jnp.float32),
            pltpu.VMEM((8, 8, LANES), jnp.float32),
            pltpu.VMEM((2, 2, LANES), jnp.float32),
            pltpu.VMEM((groups - 1, 2, 2, LANES), jnp.float32),
            pltpu.VMEM((2, groups, 2, LANES), jnp.float32),
            pltpu.VMEM((2, 4, LANES), jnp.float32),
            pltpu.VMEM((2, 4, LANES), jnp.float32),
            pltpu.VMEM((2, 1, LANES), jnp.float32),
            pltpu.VMEM((2, 1, LANES), jnp.float32),
            dma((groups - 1,)),
            dma((groups - 1,)),
            dma((2, groups)),
            dma((2, groups)),
            dma((2,)),
            dma((2,)),
            dma((2,)),
            dma((2,)),
            dma((2,)),
            dma((2,)),
        ],
        compiler_params=pltpu.CompilerParams(collective_id=0, has_side_effects=True),
    )(conn, elem_ops, resid7, interp73.T, interp31.T)
    return pl.pallas_call(
        prolong_kernel,
        out_shape=jax.ShapeDtypeStruct((64, 128), jnp.float32),
        in_specs=[VMEM, SMEM],
        out_specs=VMEM,
    )(pltpu.with_memory_space_constraint(picked, pltpu.VMEM), interp31.T)


def dispatch(resid7, interp73, interp31, elem_ops, conn, faces):
    if conn.shape[1] == LINE and resid7.shape[1] == 128 and lax.axis_size("grp") > 1:
        return one_layer(resid7, interp73, interp31, elem_ops, conn)
    return local(resid7, interp73, interp31, elem_ops, conn, faces)


def solution(mesh):
    in_specs = (
        P(None, ("slab", "grp")),
        P(),
        P(),
        P(None, None, "slab"),
        P(None, "slab"),
        P(None, "slab", None),
    )
    out_specs = P(None, ("slab", "grp"))
    return jax.shard_map(dispatch, mesh=mesh, in_specs=in_specs, out_specs=out_specs, check_vma=False)
```

```python
import functools

import jax
import jax.numpy as jnp
from jax import lax
from jax.experimental import pallas as pl
from jax.experimental.pallas import tpu as pltpu
from jax.sharding import PartitionSpec as P

EX = 32
EY = 16
SWEEPS = 2


lam_low = 0.3
lam_high = 1.9


def extended(array, sides, width):
    for axis, dim in sides:
        count, length = (lax.axis_size(axis), array.shape[dim])
        up = [(i, (i + 1) % count) for i in range(count - 1)]
        down = [(j, i) for i, j in up]
        last = lax.slice_in_dim(array, length - width, length, axis=dim)
        first = lax.slice_in_dim(array, 0, width, axis=dim)
        before = lax.ppermute(last, axis, up)
        after = lax.ppermute(first, axis, down)
        array = jnp.concatenate([before, array, after], axis=dim)
    return array


def restrict_high(block, interp73):
    hi = lax.Precision.HIGHEST
    width = block.shape[1]
    cube = block.reshape(8, 8, 8, width)
    cube = jnp.einsum("kc,ijkm->ijcm", interp73, cube, precision=hi)
    cube = jnp.einsum("jb,ijcm->ibcm", interp73, cube, precision=hi)
    cube = jnp.einsum("ia,ibcm->abcm", interp73, cube, precision=hi)
    return cube.reshape(64, width)


def restrict_low(block, interp31):
    hi = lax.Precision.HIGHEST
    width = block.shape[1]
    cube = block.reshape(4, 4, 4, width)
    cube = jnp.einsum("kc,ijkm->ijcm", interp31, cube, precision=hi)
    cube = jnp.einsum("jb,ijcm->ibcm", interp31, cube, precision=hi)
    cube = jnp.einsum("ia,ibcm->abcm", interp31, cube, precision=hi)
    return cube.reshape(8, width)


def prolong(coarse, interp31):
    hi = lax.Precision.HIGHEST
    width = coarse.shape[1]
    cube = coarse.reshape(2, 2, 2, width)
    cube = jnp.einsum("ck,ijkm->ijcm", interp31, cube, precision=hi)
    cube = jnp.einsum("bj,ijcm->ibcm", interp31, cube, precision=hi)
    cube = jnp.einsum("ai,ibcm->abcm", interp31, cube, precision=hi)
    return cube.reshape(64, width)


def assemble(values, conn_ids, count):
    layers = values.shape[0]
    flat = values.reshape(layers, -1).T
    summed = jax.ops.segment_sum(flat, conn_ids.reshape(-1), num_segments=count)
    return summed.T


def element_term(operators, conn_ids, field):
    return jnp.einsum("pqe,qe->pe", operators, field[conn_ids], precision=lax.Precision.HIGHEST)


def share(nodes, faces):
    lower = faces[0, 0]
    upper = faces[1, 0]
    planes = jnp.stack([nodes[:, lower], nodes[:, upper]], axis=1)
    padded = extended(planes, (("slab", 1),), 1)
    return nodes.at[:, lower].add(padded[:, 0]).at[:, upper].add(padded[:, 3])


def local(resid7, interp73, interp31, elem_ops, conn, faces):
    own = resid7.shape[1]
    slab_elems = conn.shape[1]
    layers = slab_elems // (EX * EY)
    count = (EX + 1) * (EY + 1) * (layers + 1)
    start = lax.axis_index("grp") * own
    own_conn = lax.dynamic_slice_in_dim(conn, start, own, 1)
    middle_res = restrict_high(resid7, interp73)
    blocks = lax.all_gather(middle_res, "grp", axis=1, tiled=True)
    slab_res = restrict_low(blocks, interp31)
    pair = jnp.stack([slab_res, jnp.einsum("ppe->pe", elem_ops)])
    both_nodes = assemble(pair, conn, count)
    shared = share(both_nodes, faces)
    rhs = shared[0]
    diag = shared[1]
    theta = 0.5 * (lam_high + lam_low)
    delta = 0.5 * (lam_high - lam_low)
    sigma = theta / delta
    inverse = 1.0 / diag
    direction = inverse * rhs / theta
    solution = direction
    remain = rhs
    rho = 1.0 / sigma
    for sweep in range(SWEEPS):
        nodes = assemble(element_term(elem_ops, conn, direction)[None], conn, count)
        remain = remain - share(nodes, faces)[0]
        rho_new = 1.0 / (2.0 * sigma - rho)
        direction = rho_new * rho * direction + 2.0 * rho_new / delta * inverse * remain
        solution = solution + direction
        rho = rho_new
    return prolong(solution[own_conn], interp31)


STRIDE = EX + 1
POINTS = (EX + 1) * (EY + 1)
LANES = (POINTS + 127) // 128 * 128
LINE = EX * EY
BLOCKS = LINE // 128
MESH = pl.DeviceIdType.MESH
VMEM = pl.BlockSpec(memory_space=pltpu.VMEM)
SMEM = pl.BlockSpec(memory_space=pltpu.SMEM)


def rows_of(shape):
    return lax.broadcasted_iota(jnp.int32, shape, 0)


def spread(row, count=8):
    return jnp.broadcast_to(row, (count, row.shape[1]))


def stack_rows(rows):
    sub = rows_of((8, rows[0].shape[1]))
    out = spread(rows[0])
    for at in range(1, 8):
        out = jnp.where(sub == at, spread(rows[at]), out)
    return out


def parts_of(value):
    hi = value.astype(jnp.bfloat16).astype(jnp.float32)
    left = value - hi
    mid = left.astype(jnp.bfloat16).astype(jnp.float32)
    return jnp.concatenate([hi, mid, left - mid], axis=0).astype(jnp.bfloat16)


def join_parts(value):
    third = value.shape[0] // 3
    return value[:third] + value[third : 2 * third] + value[2 * third :]


def gather_sums(corners):
    sub = rows_of(corners.shape)
    odd, second = (sub % 2 == 1, sub // 2 % 2 == 1)
    part = jnp.where(odd, pltpu.roll(corners, 1, 1), corners)
    part = part + jnp.where(odd, pltpu.roll(part, 1, 0), pltpu.roll(part, 7, 0))
    part = jnp.where(second, pltpu.roll(part, STRIDE, 1), part)
    return part + jnp.where(second, pltpu.roll(part, 2, 0), pltpu.roll(part, 6, 0))


def corner_values(nodes):
    sub = rows_of(nodes.shape)
    part = jnp.where(sub // 2 % 2 == 1, pltpu.roll(nodes, LANES - STRIDE, 1), nodes)
    return jnp.where(sub % 2 == 1, pltpu.roll(part, LANES - 1, 1), part)


def before(ids, mine, theirs):
    column = jnp.broadcast_to(ids[theirs : theirs + 1], (128, LINE)).T
    row = spread(ids[mine : mine + 1])
    place = rows_of((8, LINE)).astype(jnp.float32)
    total = jnp.zeros((8, LINE), jnp.float32)
    for at in range(LINE // 8):
        one = column[8 * at : 8 * at + 8]
        same = jnp.concatenate([one] * BLOCKS, axis=1) == row
        total = total + jnp.where(same, place + (8.0 * at + 1.0), 0.0)
    return jnp.sum(total, axis=0, keepdims=True)


def positions(conn):
    ids = conn.astype(jnp.float32)
    own = lax.broadcasted_iota(jnp.int32, (1, LINE), 1)
    rows = []
    for theirs in (1, 2):
        found = before(ids, 0, theirs).astype(jnp.int32)
        packed = jnp.where(found > 0, found - 1 + LINE, own)
        rows += [packed[:, 128 * b : 128 * b + 128] for b in range(BLOCKS)]
    state = stack_rows(rows)
    sub = rows_of((8, 128))
    for _ in range((EX - 1).bit_length()):
        target = state % LINE
        lane, block = (target % 128, target // 128)
        got = jnp.zeros((8, 128), jnp.int32)
        for b in range(BLOCKS):
            table = jnp.where(sub < BLOCKS, spread(state[b : b + 1]), spread(state[BLOCKS + b : BLOCKS + b + 1]))
            got = jnp.where(block == b, jnp.take_along_axis(table, lane, axis=1), got)
        state = got + (state - target)
    steps = state // LINE
    return steps + STRIDE * pltpu.roll(steps, 4, 0)


def one_hot(row):
    return jnp.where(rows_of((LANES, row.shape[1])) == spread(row, LANES), 1.0, 0.0).astype(jnp.bfloat16)


def cycle_kernel(slabs, groups, conn_hbm, ops_hbm, res_hbm, i73_ref, i31_ref, out_ref, conn_ref, ops_ref, res_ref, load_sem, lex_ref, near_ref, send_ref, got_own, got_side, out_pack, in_pack, out_far, in_far, own_send, own_recv, side_send, side_recv, ops_send, ops_recv, pack_send, pack_recv, far_send, far_recv):
    slab, group = (lax.axis_index("slab"), lax.axis_index("grp"))
    down, up = (lax.rem(slab + slabs - 1, slabs), lax.rem(slab + 1, slabs))
    has = (slab > 0, slab < slabs - 1)
    to = (down, up)
    beyond = (slab > 1, slab < slabs - 2)
    skip = (lax.rem(slab + slabs - 2, slabs), lax.rem(slab + 2, slabs))

    loads = [
        pltpu.make_async_copy(source, target, load_sem.at[at])
        for at, (source, target) in enumerate(((conn_hbm, conn_ref), (res_hbm, res_ref), (ops_hbm, ops_ref)))
    ]
    for load in loads:
        load.start()

    barrier = pltpu.get_barrier_semaphore()
    peers = [lax.rem(group + k, groups) for k in range(groups)]
    for peer in peers[1:]:
        pl.semaphore_signal(barrier, inc=1, device_id=(slab, peer), device_id_type=MESH)
    for side in range(2):

        @pl.when(has[side])
        def _():
            for peer in peers:
                pl.semaphore_signal(barrier, inc=1, device_id=(to[side], peer), device_id_type=MESH)

        @pl.when(beyond[side])
        def _():
            pl.semaphore_signal(barrier, inc=1, device_id=(skip[side], group), device_id_type=MESH)

    for side in range(2):

        @pl.when(jnp.logical_not(has[side]))
        def _():
            got_side[side] = jnp.zeros(got_side.shape[1:], jnp.float32)
            in_pack[side] = jnp.where(rows_of((4, LANES)) == 3, 1.0, 0.0)
            near_ref[:, 4 * side : 4 * side + 4, :] = jnp.zeros((8, 4, LANES), jnp.float32)

        @pl.when(jnp.logical_not(beyond[side]))
        def _():
            in_far[side] = jnp.zeros((1, LANES), jnp.float32)

    loads[0].wait()
    place = positions(conn_ref[...])
    loads[1].wait()
    loads[2].wait()
    coef = [[sum(i73_ref[m, i] * i31_ref[a, m] for m in range(4)) for a in range(2)] for i in range(8)]
    along_j = [[None] * 8, [None] * 8]
    for j in range(8):
        for a in range(2):
            along_j[a][j] = sum(coef[i][a] * res_ref[64 * i + 8 * j : 64 * i + 8 * j + 8, :] for i in range(8))
    sub_tile = rows_of((8, 128))
    last = []
    for c in range(2):
        column = jnp.full((8, 128), coef[0][c], jnp.float32)
        for k in range(1, 8):
            column = jnp.where(sub_tile == k, coef[k][c], column)
        last.append(column)
    rows = []
    for a in range(2):
        for b in range(2):
            line = sum(coef[j][b] * along_j[a][j] for j in range(8))
            for c in range(2):
                rows.append(jnp.sum(last[c] * line, axis=0, keepdims=True))
    low_res = stack_rows(rows)
    lanes = pl.ds(pl.multiple_of(group * 128, 128), 128)
    diagonal = stack_rows([ops_ref[p, p : p + 1, lanes] for p in range(8)])

    mine = spread(place[0:1])
    for b in range(1, BLOCKS):
        mine = jnp.where(group == b, spread(place[b : b + 1]), mine)
    own_hot = one_hot(mine[0:1])
    both = parts_of(jnp.concatenate([low_res, diagonal], axis=0))
    both = join_parts(lax.dot_general(both, own_hot, (((1,), (1,)), ((), ())), preferred_element_type=jnp.float32))
    for at in range(2):
        nodes = gather_sums(both[8 * at : 8 * at + 8])
        for plane in range(2):
            send_ref[plane, at : at + 1, :] = nodes[4 * plane : 4 * plane + 1]

    sides = has[0].astype(jnp.int32) + has[1].astype(jnp.int32)
    far_sides = beyond[0].astype(jnp.int32) + beyond[1].astype(jnp.int32)
    pl.semaphore_wait(barrier, groups - 1 + groups * sides + far_sides)

    side_copies = [
        [
            pltpu.make_async_remote_copy(
                src_ref=send_ref.at[side],
                dst_ref=got_side.at[1 - side, k],
                send_sem=side_send.at[side, k],
                recv_sem=side_recv.at[1 - side, k],
                device_id=(to[side], peers[k]),
                device_id_type=MESH,
            )
            for k in range(groups)
        ]
        for side in range(2)
    ]
    own_copies = [
        pltpu.make_async_remote_copy(
            src_ref=send_ref,
            dst_ref=got_own.at[k - 1],
            send_sem=own_send.at[k - 1],
            recv_sem=own_recv.at[k - 1],
            device_id=(slab, peers[k]),
            device_id_type=MESH,
        )
        for k in range(1, groups)
    ]
    for side in range(2):

        @pl.when(has[side])
        def _():
            for copy in side_copies[side]:
                copy.start()

    for copy in own_copies:
        copy.start()

    sub = rows_of((8, LANES))
    hot = jnp.concatenate([one_hot(place[b : b + 1]) for b in range(BLOCKS)], axis=1)
    ops = parts_of(ops_ref[...].reshape(64, LINE))
    lex = lax.dot_general(ops, hot, (((1,), (1,)), ((), ())), preferred_element_type=jnp.float32)
    lex_ref[...] = join_parts(lex).reshape(8, 8, LANES)
    ops_copies = []
    for side in range(2):
        ops_copies.append(
            pltpu.make_async_remote_copy(
                src_ref=lex_ref.at[:, pl.ds(4 * side, 4), :],
                dst_ref=near_ref.at[:, pl.ds(4 - 4 * side, 4), :],
                send_sem=ops_send.at[side],
                recv_sem=ops_recv.at[1 - side],
                device_id=(to[side], group),
                device_id_type=MESH,
            )
        )

        @pl.when(has[side])
        def _():
            ops_copies[side].start()


    def planes(low, high):
        return jnp.where(sub < 4, spread(low), spread(high))

    fine = []
    for k in range(2):
        column = jnp.full((8, 128), i31_ref[k, 0], jnp.float32)
        for c in range(1, 4):
            column = jnp.where(sub_tile % 4 == c, i31_ref[k, c], column)
        fine.append(column)
    weights = [jnp.where(sub_tile < 4, i31_ref[j, 2 * h], i31_ref[j, 2 * h + 1]) * fine[k] for h in range(2) for j in range(2) for k in range(2)]
    for copy in own_copies:
        copy.wait_recv()
    for side in range(2):

        @pl.when(has[side])
        def _():
            for copy in side_copies[1 - side]:
                copy.wait_recv()

    sums = []
    for plane in range(2):
        total = send_ref[plane]
        for k in range(groups - 1):
            total = total + got_own[k, plane]
        extra = got_side[plane, 0]
        for k in range(1, groups):
            extra = extra + got_side[plane, k]
        sums.append(total + extra)
    rhs = planes(sums[0][0:1], sums[1][0:1])
    diag = planes(sums[0][1:2], sums[1][1:2])
    real = lax.broadcasted_iota(jnp.int32, (8, LANES), 1) < POINTS
    inverse = 1.0 / jnp.where(real, diag, 1.0)

    theta = 0.5 * (lam_high + lam_low)
    delta = 0.5 * (lam_high - lam_low)
    sigma = theta / delta
    first = inverse * rhs * (1.0 / theta)
    corners = corner_values(first)
    product = lex_ref[0] * spread(corners[0:1])
    for q in range(1, 8):
        product = product + lex_ref[q] * spread(corners[q : q + 1])
    nodes = gather_sums(product)
    pack_copies, far_copies = ([], [])
    for side in range(2):
        near, far = (4 * side, 4 - 4 * side)
        for at, value in enumerate((nodes[near : near + 1], nodes[far : far + 1], rhs[far : far + 1], diag[far : far + 1])):
            out_pack[side, at : at + 1, :] = value
        out_far[side] = nodes[near : near + 1]
        pack_copies.append(
            pltpu.make_async_remote_copy(
                src_ref=out_pack.at[side],
                dst_ref=in_pack.at[1 - side],
                send_sem=pack_send.at[side],
                recv_sem=pack_recv.at[1 - side],
                device_id=(to[side], group),
                device_id_type=MESH,
            )
        )
        far_copies.append(
            pltpu.make_async_remote_copy(
                src_ref=out_far.at[side],
                dst_ref=in_far.at[1 - side],
                send_sem=far_send.at[side],
                recv_sem=far_recv.at[1 - side],
                device_id=(skip[side], group),
                device_id_type=MESH,
            )
        )

        @pl.when(beyond[side])
        def _():
            far_copies[side].start()

        @pl.when(has[side])
        def _():
            pack_copies[side].start()

    for side in range(2):

        @pl.when(has[side])
        def _():
            ops_copies[1 - side].wait_recv()
            pack_copies[1 - side].wait_recv()

        @pl.when(beyond[side])
        def _():
            far_copies[1 - side].wait_recv()

    low, high = (in_pack[0], in_pack[1])
    far_inverse = 1.0 / jnp.where(real, planes(low[3:4], high[3:4]), 1.0)
    far_rhs = planes(low[2:3], high[2:3])
    far_first = far_inverse * far_rhs * (1.0 / theta)
    far_remain = far_rhs - planes(low[1:2] + in_far[0], high[1:2] + in_far[1])
    remain = rhs - (nodes + planes(low[0:1], high[0:1]))
    rho = 1.0 / sigma
    rho_new = 1.0 / (2.0 * sigma - rho)
    second = rho_new * rho * first + 2.0 * rho_new / delta * inverse * remain
    far_second = rho_new * rho * far_first + 2.0 * rho_new / delta * far_inverse * far_remain
    rho = rho_new
    rho_new = 1.0 / (2.0 * sigma - rho)

    corners = corner_values(second)
    ends = (jnp.where(sub < 4, far_second, second), jnp.where(sub < 4, second, far_second))
    product = lex_ref[0] * spread(corners[0:1])
    for q in range(1, 8):
        product = product + lex_ref[q] * spread(corners[q : q + 1])
    for q in range(8):
        shift = q // 2 % 2 * STRIDE + q % 2
        value = ends[q // 4]
        product = product + near_ref[q] * (pltpu.roll(value, LANES - shift, 1) if shift else value)
    remain = remain - gather_sums(product)
    third = rho_new * rho * second + 2.0 * rho_new / delta * inverse * remain
    answer = first + second + third

    picked = join_parts(jnp.dot(parts_of(corner_values(answer)), own_hot, preferred_element_type=jnp.float32))
    for h in range(2):
        for a in range(4):
            value = i31_ref[0, a] * picked[0:4] + i31_ref[1, a] * picked[4:8]
            block = sum(weights[4 * h + q] * spread(value[q : q + 1]) for q in range(4))
            out_ref[8 * (2 * a + h) : 8 * (2 * a + h) + 8, :] = block

    for copy in own_copies:
        copy.wait_send()
    for side in range(2):

        @pl.when(has[side])
        def _():
            for copy in side_copies[side]:
                copy.wait_send()
            ops_copies[side].wait_send()
            pack_copies[side].wait_send()

        @pl.when(beyond[side])
        def _():
            far_copies[side].wait_send()


def one_layer(resid7, interp73, interp31, elem_ops, conn):
    slabs, groups = (lax.axis_size("slab"), lax.axis_size("grp"))
    dma = pltpu.SemaphoreType.DMA
    return pl.pallas_call(
        functools.partial(cycle_kernel, slabs, groups),
        out_shape=pltpu.VMEM((64, 128), jnp.float32),
        in_specs=[pl.BlockSpec(memory_space=pl.ANY)] * 3 + [SMEM] * 2,
        out_specs=VMEM,
        scratch_shapes=[
            pltpu.VMEM((8, LINE), jnp.int32),
            pltpu.VMEM((8, 8, LINE), jnp.float32),
            pltpu.VMEM((512, 128), jnp.float32),
            dma((3,)),
            pltpu.VMEM((8, 8, LANES), jnp.float32),
            pltpu.VMEM((8, 8, LANES), jnp.float32),
            pltpu.VMEM((2, 2, LANES), jnp.float32),
            pltpu.VMEM((groups - 1, 2, 2, LANES), jnp.float32),
            pltpu.VMEM((2, groups, 2, LANES), jnp.float32),
            pltpu.VMEM((2, 4, LANES), jnp.float32),
            pltpu.VMEM((2, 4, LANES), jnp.float32),
            pltpu.VMEM((2, 1, LANES), jnp.float32),
            pltpu.VMEM((2, 1, LANES), jnp.float32),
            dma((groups - 1,)),
            dma((groups - 1,)),
            dma((2, groups)),
            dma((2, groups)),
            dma((2,)),
            dma((2,)),
            dma((2,)),
            dma((2,)),
            dma((2,)),
            dma((2,)),
        ],
        compiler_params=pltpu.CompilerParams(collective_id=0, has_side_effects=True),
    )(conn, elem_ops, resid7, interp73.T, interp31.T)


def dispatch(resid7, interp73, interp31, elem_ops, conn, faces):
    if conn.shape[1] == LINE and resid7.shape[1] == 128 and lax.axis_size("grp") > 1:
        return one_layer(resid7, interp73, interp31, elem_ops, conn)
    return local(resid7, interp73, interp31, elem_ops, conn, faces)


def solution(mesh):
    in_specs = (
        P(None, ("slab", "grp")),
        P(),
        P(),
        P(None, None, "slab"),
        P(None, "slab"),
        P(None, "slab", None),
    )
    out_specs = P(None, ("slab", "grp"))
    return jax.shard_map(dispatch, mesh=mesh, in_specs=in_specs, out_specs=out_specs, check_vma=False)
```

```python
import functools

import jax
import jax.numpy as jnp
from jax import lax
from jax.experimental import pallas as pl
from jax.experimental.pallas import tpu as pltpu
from jax.sharding import PartitionSpec as P

EX = 32
EY = 16
SWEEPS = 2


lam_low = 0.3
lam_high = 1.9


def extended(array, sides, width):
    for axis, dim in sides:
        count, length = (lax.axis_size(axis), array.shape[dim])
        up = [(i, (i + 1) % count) for i in range(count - 1)]
        down = [(j, i) for i, j in up]
        last = lax.slice_in_dim(array, length - width, length, axis=dim)
        first = lax.slice_in_dim(array, 0, width, axis=dim)
        before = lax.ppermute(last, axis, up)
        after = lax.ppermute(first, axis, down)
        array = jnp.concatenate([before, array, after], axis=dim)
    return array


def restrict_high(block, interp73):
    hi = lax.Precision.HIGHEST
    width = block.shape[1]
    cube = block.reshape(8, 8, 8, width)
    cube = jnp.einsum("kc,ijkm->ijcm", interp73, cube, precision=hi)
    cube = jnp.einsum("jb,ijcm->ibcm", interp73, cube, precision=hi)
    cube = jnp.einsum("ia,ibcm->abcm", interp73, cube, precision=hi)
    return cube.reshape(64, width)


def restrict_low(block, interp31):
    hi = lax.Precision.HIGHEST
    width = block.shape[1]
    cube = block.reshape(4, 4, 4, width)
    cube = jnp.einsum("kc,ijkm->ijcm", interp31, cube, precision=hi)
    cube = jnp.einsum("jb,ijcm->ibcm", interp31, cube, precision=hi)
    cube = jnp.einsum("ia,ibcm->abcm", interp31, cube, precision=hi)
    return cube.reshape(8, width)


def prolong(coarse, interp31):
    hi = lax.Precision.HIGHEST
    width = coarse.shape[1]
    cube = coarse.reshape(2, 2, 2, width)
    cube = jnp.einsum("ck,ijkm->ijcm", interp31, cube, precision=hi)
    cube = jnp.einsum("bj,ijcm->ibcm", interp31, cube, precision=hi)
    cube = jnp.einsum("ai,ibcm->abcm", interp31, cube, precision=hi)
    return cube.reshape(64, width)


def assemble(values, conn_ids, count):
    layers = values.shape[0]
    flat = values.reshape(layers, -1).T
    summed = jax.ops.segment_sum(flat, conn_ids.reshape(-1), num_segments=count)
    return summed.T


def element_term(operators, conn_ids, field):
    return jnp.einsum("pqe,qe->pe", operators, field[conn_ids], precision=lax.Precision.HIGHEST)


def share(nodes, faces):
    lower = faces[0, 0]
    upper = faces[1, 0]
    planes = jnp.stack([nodes[:, lower], nodes[:, upper]], axis=1)
    padded = extended(planes, (("slab", 1),), 1)
    return nodes.at[:, lower].add(padded[:, 0]).at[:, upper].add(padded[:, 3])


def local(resid7, interp73, interp31, elem_ops, conn, faces):
    own = resid7.shape[1]
    slab_elems = conn.shape[1]
    layers = slab_elems // (EX * EY)
    count = (EX + 1) * (EY + 1) * (layers + 1)
    start = lax.axis_index("grp") * own
    own_conn = lax.dynamic_slice_in_dim(conn, start, own, 1)
    middle_res = restrict_high(resid7, interp73)
    blocks = lax.all_gather(middle_res, "grp", axis=1, tiled=True)
    slab_res = restrict_low(blocks, interp31)
    pair = jnp.stack([slab_res, jnp.einsum("ppe->pe", elem_ops)])
    both_nodes = assemble(pair, conn, count)
    shared = share(both_nodes, faces)
    rhs = shared[0]
    diag = shared[1]
    theta = 0.5 * (lam_high + lam_low)
    delta = 0.5 * (lam_high - lam_low)
    sigma = theta / delta
    inverse = 1.0 / diag
    direction = inverse * rhs / theta
    solution = direction
    remain = rhs
    rho = 1.0 / sigma
    for sweep in range(SWEEPS):
        nodes = assemble(element_term(elem_ops, conn, direction)[None], conn, count)
        remain = remain - share(nodes, faces)[0]
        rho_new = 1.0 / (2.0 * sigma - rho)
        direction = rho_new * rho * direction + 2.0 * rho_new / delta * inverse * remain
        solution = solution + direction
        rho = rho_new
    return prolong(solution[own_conn], interp31)


STRIDE = EX + 1
POINTS = (EX + 1) * (EY + 1)
LANES = (POINTS + 127) // 128 * 128
LINE = EX * EY
BLOCKS = LINE // 128
MESH = pl.DeviceIdType.MESH
VMEM = pl.BlockSpec(memory_space=pltpu.VMEM)
SMEM = pl.BlockSpec(memory_space=pltpu.SMEM)


def rows_of(shape):
    return lax.broadcasted_iota(jnp.int32, shape, 0)


def spread(row, count=8):
    return jnp.broadcast_to(row, (count, row.shape[1]))


def stack_rows(rows):
    sub = rows_of((8, rows[0].shape[1]))
    out = spread(rows[0])
    for at in range(1, 8):
        out = jnp.where(sub == at, spread(rows[at]), out)
    return out


def parts_of(value):
    hi = value.astype(jnp.bfloat16).astype(jnp.float32)
    left = value - hi
    mid = left.astype(jnp.bfloat16).astype(jnp.float32)
    return jnp.concatenate([hi, mid, left - mid], axis=0).astype(jnp.bfloat16)


def join_parts(value):
    third = value.shape[0] // 3
    return value[:third] + value[third : 2 * third] + value[2 * third :]


def gather_sums(corners):
    sub = rows_of(corners.shape)
    odd, second = ((sub & 1) == 1, (sub & 2) == 2)
    part = jnp.where(odd, pltpu.roll(corners, 1, 1), corners)
    part = part + jnp.where(odd, pltpu.roll(part, 1, 0), pltpu.roll(part, 7, 0))
    part = jnp.where(second, pltpu.roll(part, STRIDE, 1), part)
    return part + jnp.where(second, pltpu.roll(part, 2, 0), pltpu.roll(part, 6, 0))


def corner_values(nodes):
    sub = rows_of(nodes.shape)
    part = jnp.where((sub & 2) == 2, pltpu.roll(nodes, LANES - STRIDE, 1), nodes)
    return jnp.where((sub & 1) == 1, pltpu.roll(part, LANES - 1, 1), part)


def before(ids, mine, theirs):
    column = jnp.broadcast_to(ids[theirs : theirs + 1], (128, LINE)).T
    row = spread(ids[mine : mine + 1])
    place = rows_of((8, LINE)).astype(jnp.float32)
    total = jnp.zeros((8, LINE), jnp.float32)
    for at in range(LINE // 8):
        one = column[8 * at : 8 * at + 8]
        same = jnp.concatenate([one] * BLOCKS, axis=1) == row
        total = total + jnp.where(same, place + (8.0 * at + 1.0), 0.0)
    return jnp.sum(total, axis=0, keepdims=True)


def positions(conn):
    ids = conn.astype(jnp.float32)
    own = lax.broadcasted_iota(jnp.int32, (1, LINE), 1)
    rows = []
    for theirs in (1, 2):
        found = before(ids, 0, theirs).astype(jnp.int32)
        packed = jnp.where(found > 0, found - 1 + LINE, own)
        rows += [packed[:, 128 * b : 128 * b + 128] for b in range(BLOCKS)]
    state = stack_rows(rows)
    sub = rows_of((8, 128))
    for _ in range((EX - 1).bit_length()):
        target = state & (LINE - 1)
        lane, block = (target & 127, target >> 7)
        got = jnp.zeros((8, 128), jnp.int32)
        for b in range(BLOCKS):
            table = jnp.where(sub < BLOCKS, spread(state[b : b + 1]), spread(state[BLOCKS + b : BLOCKS + b + 1]))
            got = jnp.where(block == b, jnp.take_along_axis(table, lane, axis=1), got)
        state = got + (state - target)
    steps = state >> (LINE.bit_length() - 1)
    return steps + STRIDE * pltpu.roll(steps, 4, 0)


def one_hot(row):
    return jnp.where(rows_of((LANES, row.shape[1])) == spread(row, LANES), 1.0, 0.0).astype(jnp.bfloat16)


def cycle_kernel(slabs, groups, conn_hbm, ops_hbm, res_hbm, i73_ref, i31_ref, out_ref, conn_ref, ops_ref, res_ref, load_sem, lex_ref, near_ref, send_ref, got_own, got_side, out_pack, in_pack, out_far, in_far, own_send, own_recv, side_send, side_recv, ops_send, ops_recv, pack_send, pack_recv, far_send, far_recv):
    slab, group = (lax.axis_index("slab"), lax.axis_index("grp"))
    down, up = (lax.rem(slab + slabs - 1, slabs), lax.rem(slab + 1, slabs))
    has = (slab > 0, slab < slabs - 1)
    to = (down, up)
    beyond = (slab > 1, slab < slabs - 2)
    skip = (lax.rem(slab + slabs - 2, slabs), lax.rem(slab + 2, slabs))

    loads = [
        pltpu.make_async_copy(source, target, load_sem.at[at])
        for at, (source, target) in enumerate(((conn_hbm, conn_ref), (res_hbm, res_ref), (ops_hbm, ops_ref)))
    ]
    for load in loads:
        load.start()

    barrier = pltpu.get_barrier_semaphore()
    peers = [lax.rem(group + k, groups) for k in range(groups)]
    for peer in peers[1:]:
        pl.semaphore_signal(barrier, inc=1, device_id=(slab, peer), device_id_type=MESH)
    for side in range(2):

        @pl.when(has[side])
        def _():
            for peer in peers:
                pl.semaphore_signal(barrier, inc=1, device_id=(to[side], peer), device_id_type=MESH)

        @pl.when(beyond[side])
        def _():
            pl.semaphore_signal(barrier, inc=1, device_id=(skip[side], group), device_id_type=MESH)

    for side in range(2):

        @pl.when(jnp.logical_not(has[side]))
        def _():
            got_side[side] = jnp.zeros(got_side.shape[1:], jnp.float32)
            in_pack[side] = jnp.where(rows_of((4, LANES)) == 3, 1.0, 0.0)
            near_ref[:, 4 * side : 4 * side + 4, :] = jnp.zeros((8, 4, LANES), jnp.float32)

        @pl.when(jnp.logical_not(beyond[side]))
        def _():
            in_far[side] = jnp.zeros((1, LANES), jnp.float32)

    loads[0].wait()
    place = positions(conn_ref[...])
    loads[1].wait()
    loads[2].wait()
    coef = [[sum(i73_ref[m, i] * i31_ref[a, m] for m in range(4)) for a in range(2)] for i in range(8)]
    along_j = [[None] * 8, [None] * 8]
    for j in range(8):
        for a in range(2):
            along_j[a][j] = sum(coef[i][a] * res_ref[64 * i + 8 * j : 64 * i + 8 * j + 8, :] for i in range(8))
    sub_tile = rows_of((8, 128))
    last = []
    for c in range(2):
        column = jnp.full((8, 128), coef[0][c], jnp.float32)
        for k in range(1, 8):
            column = jnp.where(sub_tile == k, coef[k][c], column)
        last.append(column)
    rows = []
    for a in range(2):
        for b in range(2):
            line = sum(coef[j][b] * along_j[a][j] for j in range(8))
            for c in range(2):
                rows.append(jnp.sum(last[c] * line, axis=0, keepdims=True))
    low_res = stack_rows(rows)
    lanes = pl.ds(pl.multiple_of(group * 128, 128), 128)
    diagonal = stack_rows([ops_ref[p, p : p + 1, lanes] for p in range(8)])

    mine = spread(place[0:1])
    for b in range(1, BLOCKS):
        mine = jnp.where(group == b, spread(place[b : b + 1]), mine)
    own_hot = one_hot(mine[0:1])
    both = parts_of(jnp.concatenate([low_res, diagonal], axis=0))
    both = join_parts(lax.dot_general(both, own_hot, (((1,), (1,)), ((), ())), preferred_element_type=jnp.float32))
    for at in range(2):
        nodes = gather_sums(both[8 * at : 8 * at + 8])
        for plane in range(2):
            send_ref[plane, at : at + 1, :] = nodes[4 * plane : 4 * plane + 1]

    sides = has[0].astype(jnp.int32) + has[1].astype(jnp.int32)
    far_sides = beyond[0].astype(jnp.int32) + beyond[1].astype(jnp.int32)
    pl.semaphore_wait(barrier, groups - 1 + groups * sides + far_sides)

    side_copies = [
        [
            pltpu.make_async_remote_copy(
                src_ref=send_ref.at[side],
                dst_ref=got_side.at[1 - side, k],
                send_sem=side_send.at[side, k],
                recv_sem=side_recv.at[1 - side, k],
                device_id=(to[side], peers[k]),
                device_id_type=MESH,
            )
            for k in range(groups)
        ]
        for side in range(2)
    ]
    own_copies = [
        pltpu.make_async_remote_copy(
            src_ref=send_ref,
            dst_ref=got_own.at[k - 1],
            send_sem=own_send.at[k - 1],
            recv_sem=own_recv.at[k - 1],
            device_id=(slab, peers[k]),
            device_id_type=MESH,
        )
        for k in range(1, groups)
    ]
    for side in range(2):

        @pl.when(has[side])
        def _():
            for copy in side_copies[side]:
                copy.start()

    for copy in own_copies:
        copy.start()

    sub = rows_of((8, LANES))
    hot = jnp.concatenate([one_hot(place[b : b + 1]) for b in range(BLOCKS)], axis=1)
    ops = parts_of(ops_ref[...].reshape(64, LINE))
    lex = lax.dot_general(ops, hot, (((1,), (1,)), ((), ())), preferred_element_type=jnp.float32)
    lex_ref[...] = join_parts(lex).reshape(8, 8, LANES)
    ops_copies = []
    for side in range(2):
        ops_copies.append(
            pltpu.make_async_remote_copy(
                src_ref=lex_ref.at[:, pl.ds(4 * side, 4), :],
                dst_ref=near_ref.at[:, pl.ds(4 - 4 * side, 4), :],
                send_sem=ops_send.at[side],
                recv_sem=ops_recv.at[1 - side],
                device_id=(to[side], group),
                device_id_type=MESH,
            )
        )

        @pl.when(has[side])
        def _():
            ops_copies[side].start()


    def planes(low, high):
        return jnp.where(sub < 4, spread(low), spread(high))

    fine = []
    for k in range(2):
        column = jnp.full((8, 128), i31_ref[k, 0], jnp.float32)
        for c in range(1, 4):
            column = jnp.where((sub_tile & 3) == c, i31_ref[k, c], column)
        fine.append(column)
    weights = [jnp.where(sub_tile < 4, i31_ref[j, 2 * h], i31_ref[j, 2 * h + 1]) * fine[k] for h in range(2) for j in range(2) for k in range(2)]
    for copy in own_copies:
        copy.wait_recv()
    for side in range(2):

        @pl.when(has[side])
        def _():
            for copy in side_copies[1 - side]:
                copy.wait_recv()

    sums = []
    for plane in range(2):
        total = send_ref[plane]
        for k in range(groups - 1):
            total = total + got_own[k, plane]
        extra = got_side[plane, 0]
        for k in range(1, groups):
            extra = extra + got_side[plane, k]
        sums.append(total + extra)
    rhs = planes(sums[0][0:1], sums[1][0:1])
    diag = planes(sums[0][1:2], sums[1][1:2])
    real = lax.broadcasted_iota(jnp.int32, (8, LANES), 1) < POINTS
    inverse = 1.0 / jnp.where(real, diag, 1.0)

    theta = 0.5 * (lam_high + lam_low)
    delta = 0.5 * (lam_high - lam_low)
    sigma = theta / delta
    first = inverse * rhs * (1.0 / theta)
    corners = corner_values(first)
    product = lex_ref[0] * spread(corners[0:1])
    for q in range(1, 8):
        product = product + lex_ref[q] * spread(corners[q : q + 1])
    nodes = gather_sums(product)
    pack_copies, far_copies = ([], [])
    for side in range(2):
        near, far = (4 * side, 4 - 4 * side)
        for at, value in enumerate((nodes[near : near + 1], nodes[far : far + 1], rhs[far : far + 1], diag[far : far + 1])):
            out_pack[side, at : at + 1, :] = value
        out_far[side] = nodes[near : near + 1]
        pack_copies.append(
            pltpu.make_async_remote_copy(
                src_ref=out_pack.at[side],
                dst_ref=in_pack.at[1 - side],
                send_sem=pack_send.at[side],
                recv_sem=pack_recv.at[1 - side],
                device_id=(to[side], group),
                device_id_type=MESH,
            )
        )
        far_copies.append(
            pltpu.make_async_remote_copy(
                src_ref=out_far.at[side],
                dst_ref=in_far.at[1 - side],
                send_sem=far_send.at[side],
                recv_sem=far_recv.at[1 - side],
                device_id=(skip[side], group),
                device_id_type=MESH,
            )
        )

        @pl.when(beyond[side])
        def _():
            far_copies[side].start()

        @pl.when(has[side])
        def _():
            pack_copies[side].start()

    for side in range(2):

        @pl.when(has[side])
        def _():
            ops_copies[1 - side].wait_recv()
            pack_copies[1 - side].wait_recv()

        @pl.when(beyond[side])
        def _():
            far_copies[1 - side].wait_recv()

    low, high = (in_pack[0], in_pack[1])
    far_inverse = 1.0 / jnp.where(real, planes(low[3:4], high[3:4]), 1.0)
    far_rhs = planes(low[2:3], high[2:3])
    far_first = far_inverse * far_rhs * (1.0 / theta)
    far_remain = far_rhs - planes(low[1:2] + in_far[0], high[1:2] + in_far[1])
    remain = rhs - (nodes + planes(low[0:1], high[0:1]))
    rho = 1.0 / sigma
    rho_new = 1.0 / (2.0 * sigma - rho)
    second = rho_new * rho * first + 2.0 * rho_new / delta * inverse * remain
    far_second = rho_new * rho * far_first + 2.0 * rho_new / delta * far_inverse * far_remain
    rho = rho_new
    rho_new = 1.0 / (2.0 * sigma - rho)

    corners = corner_values(second)
    ends = (jnp.where(sub < 4, far_second, second), jnp.where(sub < 4, second, far_second))
    product = lex_ref[0] * spread(corners[0:1])
    for q in range(1, 8):
        product = product + lex_ref[q] * spread(corners[q : q + 1])
    for q in range(8):
        shift = q // 2 % 2 * STRIDE + q % 2
        value = ends[q // 4]
        product = product + near_ref[q] * (pltpu.roll(value, LANES - shift, 1) if shift else value)
    remain = remain - gather_sums(product)
    third = rho_new * rho * second + 2.0 * rho_new / delta * inverse * remain
    answer = first + second + third

    picked = join_parts(jnp.dot(parts_of(corner_values(answer)), own_hot, preferred_element_type=jnp.float32))
    for h in range(2):
        for a in range(4):
            value = i31_ref[0, a] * picked[0:4] + i31_ref[1, a] * picked[4:8]
            block = sum(weights[4 * h + q] * spread(value[q : q + 1]) for q in range(4))
            out_ref[8 * (2 * a + h) : 8 * (2 * a + h) + 8, :] = block

    for copy in own_copies:
        copy.wait_send()
    for side in range(2):

        @pl.when(has[side])
        def _():
            for copy in side_copies[side]:
                copy.wait_send()
            ops_copies[side].wait_send()
            pack_copies[side].wait_send()

        @pl.when(beyond[side])
        def _():
            far_copies[side].wait_send()


def one_layer(resid7, interp73, interp31, elem_ops, conn):
    slabs, groups = (lax.axis_size("slab"), lax.axis_size("grp"))
    dma = pltpu.SemaphoreType.DMA
    return pl.pallas_call(
        functools.partial(cycle_kernel, slabs, groups),
        out_shape=pltpu.VMEM((64, 128), jnp.float32),
        in_specs=[pl.BlockSpec(memory_space=pl.ANY)] * 3 + [SMEM] * 2,
        out_specs=VMEM,
        scratch_shapes=[
            pltpu.VMEM((8, LINE), jnp.int32),
            pltpu.VMEM((8, 8, LINE), jnp.float32),
            pltpu.VMEM((512, 128), jnp.float32),
            dma((3,)),
            pltpu.VMEM((8, 8, LANES), jnp.float32),
            pltpu.VMEM((8, 8, LANES), jnp.float32),
            pltpu.VMEM((2, 2, LANES), jnp.float32),
            pltpu.VMEM((groups - 1, 2, 2, LANES), jnp.float32),
            pltpu.VMEM((2, groups, 2, LANES), jnp.float32),
            pltpu.VMEM((2, 4, LANES), jnp.float32),
            pltpu.VMEM((2, 4, LANES), jnp.float32),
            pltpu.VMEM((2, 1, LANES), jnp.float32),
            pltpu.VMEM((2, 1, LANES), jnp.float32),
            dma((groups - 1,)),
            dma((groups - 1,)),
            dma((2, groups)),
            dma((2, groups)),
            dma((2,)),
            dma((2,)),
            dma((2,)),
            dma((2,)),
            dma((2,)),
            dma((2,)),
        ],
        compiler_params=pltpu.CompilerParams(collective_id=0, has_side_effects=True),
    )(conn, elem_ops, resid7, interp73.T, interp31.T)


def dispatch(resid7, interp73, interp31, elem_ops, conn, faces):
    if conn.shape[1] == LINE and resid7.shape[1] == 128 and lax.axis_size("grp") > 1:
        return one_layer(resid7, interp73, interp31, elem_ops, conn)
    return local(resid7, interp73, interp31, elem_ops, conn, faces)


def solution(mesh):
    in_specs = (
        P(None, ("slab", "grp")),
        P(),
        P(),
        P(None, None, "slab"),
        P(None, "slab"),
        P(None, "slab", None),
    )
    out_specs = P(None, ("slab", "grp"))
    return jax.shard_map(dispatch, mesh=mesh, in_specs=in_specs, out_specs=out_specs, check_vma=False)
```

```python
import functools

import jax
import jax.numpy as jnp
from jax import lax
from jax.experimental import pallas as pl
from jax.experimental.pallas import tpu as pltpu
from jax.sharding import PartitionSpec as P

EX = 32
EY = 16
SWEEPS = 2


lam_low = 0.3
lam_high = 1.9


def extended(array, sides, width):
    for axis, dim in sides:
        count, length = (lax.axis_size(axis), array.shape[dim])
        up = [(i, (i + 1) % count) for i in range(count - 1)]
        down = [(j, i) for i, j in up]
        last = lax.slice_in_dim(array, length - width, length, axis=dim)
        first = lax.slice_in_dim(array, 0, width, axis=dim)
        before = lax.ppermute(last, axis, up)
        after = lax.ppermute(first, axis, down)
        array = jnp.concatenate([before, array, after], axis=dim)
    return array


def restrict_high(block, interp73):
    hi = lax.Precision.HIGHEST
    width = block.shape[1]
    cube = block.reshape(8, 8, 8, width)
    cube = jnp.einsum("kc,ijkm->ijcm", interp73, cube, precision=hi)
    cube = jnp.einsum("jb,ijcm->ibcm", interp73, cube, precision=hi)
    cube = jnp.einsum("ia,ibcm->abcm", interp73, cube, precision=hi)
    return cube.reshape(64, width)


def restrict_low(block, interp31):
    hi = lax.Precision.HIGHEST
    width = block.shape[1]
    cube = block.reshape(4, 4, 4, width)
    cube = jnp.einsum("kc,ijkm->ijcm", interp31, cube, precision=hi)
    cube = jnp.einsum("jb,ijcm->ibcm", interp31, cube, precision=hi)
    cube = jnp.einsum("ia,ibcm->abcm", interp31, cube, precision=hi)
    return cube.reshape(8, width)


def prolong(coarse, interp31):
    hi = lax.Precision.HIGHEST
    width = coarse.shape[1]
    cube = coarse.reshape(2, 2, 2, width)
    cube = jnp.einsum("ck,ijkm->ijcm", interp31, cube, precision=hi)
    cube = jnp.einsum("bj,ijcm->ibcm", interp31, cube, precision=hi)
    cube = jnp.einsum("ai,ibcm->abcm", interp31, cube, precision=hi)
    return cube.reshape(64, width)


def assemble(values, conn_ids, count):
    layers = values.shape[0]
    flat = values.reshape(layers, -1).T
    summed = jax.ops.segment_sum(flat, conn_ids.reshape(-1), num_segments=count)
    return summed.T


def element_term(operators, conn_ids, field):
    return jnp.einsum("pqe,qe->pe", operators, field[conn_ids], precision=lax.Precision.HIGHEST)


def share(nodes, faces):
    lower = faces[0, 0]
    upper = faces[1, 0]
    planes = jnp.stack([nodes[:, lower], nodes[:, upper]], axis=1)
    padded = extended(planes, (("slab", 1),), 1)
    return nodes.at[:, lower].add(padded[:, 0]).at[:, upper].add(padded[:, 3])


def local(resid7, interp73, interp31, elem_ops, conn, faces):
    own = resid7.shape[1]
    slab_elems = conn.shape[1]
    layers = slab_elems // (EX * EY)
    count = (EX + 1) * (EY + 1) * (layers + 1)
    start = lax.axis_index("grp") * own
    own_conn = lax.dynamic_slice_in_dim(conn, start, own, 1)
    middle_res = restrict_high(resid7, interp73)
    blocks = lax.all_gather(middle_res, "grp", axis=1, tiled=True)
    slab_res = restrict_low(blocks, interp31)
    pair = jnp.stack([slab_res, jnp.einsum("ppe->pe", elem_ops)])
    both_nodes = assemble(pair, conn, count)
    shared = share(both_nodes, faces)
    rhs = shared[0]
    diag = shared[1]
    theta = 0.5 * (lam_high + lam_low)
    delta = 0.5 * (lam_high - lam_low)
    sigma = theta / delta
    inverse = 1.0 / diag
    direction = inverse * rhs / theta
    solution = direction
    remain = rhs
    rho = 1.0 / sigma
    for sweep in range(SWEEPS):
        nodes = assemble(element_term(elem_ops, conn, direction)[None], conn, count)
        remain = remain - share(nodes, faces)[0]
        rho_new = 1.0 / (2.0 * sigma - rho)
        direction = rho_new * rho * direction + 2.0 * rho_new / delta * inverse * remain
        solution = solution + direction
        rho = rho_new
    return prolong(solution[own_conn], interp31)


STRIDE = EX + 1
POINTS = (EX + 1) * (EY + 1)
LANES = (POINTS + 127) // 128 * 128
LINE = EX * EY
BLOCKS = LINE // 128
MESH = pl.DeviceIdType.MESH
VMEM = pl.BlockSpec(memory_space=pltpu.VMEM)
SMEM = pl.BlockSpec(memory_space=pltpu.SMEM)


def rows_of(shape):
    return lax.broadcasted_iota(jnp.int32, shape, 0)


def spread(row, count=8):
    return jnp.broadcast_to(row, (count, row.shape[1]))


def stack_rows(rows):
    sub = rows_of((8, rows[0].shape[1]))
    out = spread(rows[0])
    for at in range(1, 8):
        out = jnp.where(sub == at, spread(rows[at]), out)
    return out


def parts_of(value):
    hi = value.astype(jnp.bfloat16).astype(jnp.float32)
    left = value - hi
    mid = left.astype(jnp.bfloat16).astype(jnp.float32)
    return jnp.concatenate([hi, mid, left - mid], axis=0).astype(jnp.bfloat16)


def join_parts(value):
    third = value.shape[0] // 3
    return value[:third] + value[third : 2 * third] + value[2 * third :]


def gather_sums(corners):
    sub = rows_of(corners.shape)
    odd, second = ((sub & 1) == 1, (sub & 2) == 2)
    part = jnp.where(odd, pltpu.roll(corners, 1, 1), corners)
    part = part + jnp.where(odd, pltpu.roll(part, 1, 0), pltpu.roll(part, 7, 0))
    part = jnp.where(second, pltpu.roll(part, STRIDE, 1), part)
    return part + jnp.where(second, pltpu.roll(part, 2, 0), pltpu.roll(part, 6, 0))


def corner_values(nodes):
    sub = rows_of(nodes.shape)
    part = jnp.where((sub & 2) == 2, pltpu.roll(nodes, LANES - STRIDE, 1), nodes)
    return jnp.where((sub & 1) == 1, pltpu.roll(part, LANES - 1, 1), part)


def before(ids, mine, theirs):
    column = jnp.broadcast_to(ids[theirs : theirs + 1], (128, LINE)).T
    row = spread(ids[mine : mine + 1])
    place = rows_of((8, LINE)).astype(jnp.float32)
    total = jnp.zeros((8, LINE), jnp.float32)
    for at in range(LINE // 8):
        one = column[8 * at : 8 * at + 8]
        same = jnp.concatenate([one] * BLOCKS, axis=1) == row
        total = total + jnp.where(same, place + (8.0 * at + 1.0), 0.0)
    return jnp.sum(total, axis=0, keepdims=True)


def positions(conn):
    ids = conn.astype(jnp.float32)
    own = lax.broadcasted_iota(jnp.int32, (1, LINE), 1)
    rows = []
    for theirs in (1, 2):
        found = before(ids, 0, theirs).astype(jnp.int32)
        packed = jnp.where(found > 0, found - 1 + LINE, own)
        rows += [packed[:, 128 * b : 128 * b + 128] for b in range(BLOCKS)]
    state = stack_rows(rows)
    sub = rows_of((8, 128))
    for _ in range((EX - 1).bit_length()):
        target = state & (LINE - 1)
        lane, block = (target & 127, target >> 7)
        got = jnp.zeros((8, 128), jnp.int32)
        for b in range(BLOCKS):
            table = jnp.where(sub < BLOCKS, spread(state[b : b + 1]), spread(state[BLOCKS + b : BLOCKS + b + 1]))
            got = jnp.where(block == b, jnp.take_along_axis(table, lane, axis=1), got)
        state = got + (state - target)
    steps = state >> (LINE.bit_length() - 1)
    return steps + STRIDE * pltpu.roll(steps, 4, 0)


def one_hot(row):
    return jnp.where(rows_of((LANES, row.shape[1])) == spread(row, LANES), 1.0, 0.0).astype(jnp.bfloat16)


def cycle_kernel(slabs, groups, conn_hbm, ops_hbm, res_hbm, i73_ref, i31_ref, out_ref, conn_ref, ops_ref, res_ref, load_sem, lex_ref, near_ref, send_ref, got_own, got_side, out_pack, in_pack, out_far, in_far, own_send, own_recv, side_send, side_recv, ops_send, ops_recv, pack_send, pack_recv, far_send, far_recv, out_early, in_early, early_send, early_recv):
    slab, group = (lax.axis_index("slab"), lax.axis_index("grp"))
    down, up = (lax.rem(slab + slabs - 1, slabs), lax.rem(slab + 1, slabs))
    has = (slab > 0, slab < slabs - 1)
    to = (down, up)
    beyond = (slab > 1, slab < slabs - 2)
    skip = (lax.rem(slab + slabs - 2, slabs), lax.rem(slab + 2, slabs))

    loads = [
        pltpu.make_async_copy(source, target, load_sem.at[at])
        for at, (source, target) in enumerate(((conn_hbm, conn_ref), (res_hbm, res_ref), (ops_hbm, ops_ref)))
    ]
    for load in loads:
        load.start()

    barrier = pltpu.get_barrier_semaphore()
    peers = [lax.rem(group + k, groups) for k in range(groups)]
    for peer in peers[1:]:
        pl.semaphore_signal(barrier, inc=1, device_id=(slab, peer), device_id_type=MESH)
    for side in range(2):

        @pl.when(has[side])
        def _():
            for peer in peers:
                pl.semaphore_signal(barrier, inc=1, device_id=(to[side], peer), device_id_type=MESH)

        @pl.when(beyond[side])
        def _():
            pl.semaphore_signal(barrier, inc=1, device_id=(skip[side], group), device_id_type=MESH)

    for side in range(2):

        @pl.when(jnp.logical_not(has[side]))
        def _():
            got_side[side] = jnp.zeros(got_side.shape[1:], jnp.float32)
            in_pack[side] = jnp.zeros((2, LANES), jnp.float32)
            in_early[side] = jnp.where(rows_of((2, LANES)) == 1, 1.0, 0.0)
            near_ref[:, 4 * side : 4 * side + 4, :] = jnp.zeros((8, 4, LANES), jnp.float32)

        @pl.when(jnp.logical_not(beyond[side]))
        def _():
            in_far[side] = jnp.zeros((1, LANES), jnp.float32)

    loads[0].wait()
    place = positions(conn_ref[...])
    loads[1].wait()
    loads[2].wait()
    coef = [[sum(i73_ref[m, i] * i31_ref[a, m] for m in range(4)) for a in range(2)] for i in range(8)]
    along_j = [[None] * 8, [None] * 8]
    for j in range(8):
        for a in range(2):
            along_j[a][j] = sum(coef[i][a] * res_ref[64 * i + 8 * j : 64 * i + 8 * j + 8, :] for i in range(8))
    sub_tile = rows_of((8, 128))
    last = []
    for c in range(2):
        column = jnp.full((8, 128), coef[0][c], jnp.float32)
        for k in range(1, 8):
            column = jnp.where(sub_tile == k, coef[k][c], column)
        last.append(column)
    rows = []
    for a in range(2):
        for b in range(2):
            line = sum(coef[j][b] * along_j[a][j] for j in range(8))
            for c in range(2):
                rows.append(jnp.sum(last[c] * line, axis=0, keepdims=True))
    low_res = stack_rows(rows)
    lanes = pl.ds(pl.multiple_of(group * 128, 128), 128)
    diagonal = stack_rows([ops_ref[p, p : p + 1, lanes] for p in range(8)])

    mine = spread(place[0:1])
    for b in range(1, BLOCKS):
        mine = jnp.where(group == b, spread(place[b : b + 1]), mine)
    own_hot = one_hot(mine[0:1])
    both = parts_of(jnp.concatenate([low_res, diagonal], axis=0))
    both = join_parts(lax.dot_general(both, own_hot, (((1,), (1,)), ((), ())), preferred_element_type=jnp.float32))
    for at in range(2):
        nodes = gather_sums(both[8 * at : 8 * at + 8])
        for plane in range(2):
            send_ref[plane, at : at + 1, :] = nodes[4 * plane : 4 * plane + 1]

    sides = has[0].astype(jnp.int32) + has[1].astype(jnp.int32)
    far_sides = beyond[0].astype(jnp.int32) + beyond[1].astype(jnp.int32)
    pl.semaphore_wait(barrier, groups - 1 + groups * sides + far_sides)

    side_copies = [
        [
            pltpu.make_async_remote_copy(
                src_ref=send_ref.at[side],
                dst_ref=got_side.at[1 - side, k],
                send_sem=side_send.at[side, k],
                recv_sem=side_recv.at[1 - side, k],
                device_id=(to[side], peers[k]),
                device_id_type=MESH,
            )
            for k in range(groups)
        ]
        for side in range(2)
    ]
    own_copies = [
        pltpu.make_async_remote_copy(
            src_ref=send_ref,
            dst_ref=got_own.at[k - 1],
            send_sem=own_send.at[k - 1],
            recv_sem=own_recv.at[k - 1],
            device_id=(slab, peers[k]),
            device_id_type=MESH,
        )
        for k in range(1, groups)
    ]
    for side in range(2):

        @pl.when(has[side])
        def _():
            for copy in side_copies[side]:
                copy.start()

    for copy in own_copies:
        copy.start()

    sub = rows_of((8, LANES))
    hot = jnp.concatenate([one_hot(place[b : b + 1]) for b in range(BLOCKS)], axis=1)
    ops = parts_of(ops_ref[...].reshape(64, LINE))
    lex = lax.dot_general(ops, hot, (((1,), (1,)), ((), ())), preferred_element_type=jnp.float32)
    lex_ref[...] = join_parts(lex).reshape(8, 8, LANES)
    ops_copies = []
    for side in range(2):
        ops_copies.append(
            pltpu.make_async_remote_copy(
                src_ref=lex_ref.at[:, pl.ds(4 * side, 4), :],
                dst_ref=near_ref.at[:, pl.ds(4 - 4 * side, 4), :],
                send_sem=ops_send.at[side],
                recv_sem=ops_recv.at[1 - side],
                device_id=(to[side], group),
                device_id_type=MESH,
            )
        )

        @pl.when(has[side])
        def _():
            ops_copies[side].start()


    def planes(low, high):
        return jnp.where(sub < 4, spread(low), spread(high))

    fine = []
    for k in range(2):
        column = jnp.full((8, 128), i31_ref[k, 0], jnp.float32)
        for c in range(1, 4):
            column = jnp.where((sub_tile & 3) == c, i31_ref[k, c], column)
        fine.append(column)
    weights = [jnp.where(sub_tile < 4, i31_ref[j, 2 * h], i31_ref[j, 2 * h + 1]) * fine[k] for h in range(2) for j in range(2) for k in range(2)]
    for copy in own_copies:
        copy.wait_recv()
    for side in range(2):

        @pl.when(has[side])
        def _():
            for copy in side_copies[1 - side]:
                copy.wait_recv()

    sums = []
    for plane in range(2):
        total = send_ref[plane]
        for k in range(groups - 1):
            total = total + got_own[k, plane]
        extra = got_side[plane, 0]
        for k in range(1, groups):
            extra = extra + got_side[plane, k]
        sums.append(total + extra)
    rhs = planes(sums[0][0:1], sums[1][0:1])
    diag = planes(sums[0][1:2], sums[1][1:2])
    real = lax.broadcasted_iota(jnp.int32, (8, LANES), 1) < POINTS
    inverse = 1.0 / jnp.where(real, diag, 1.0)

    theta = 0.5 * (lam_high + lam_low)
    delta = 0.5 * (lam_high - lam_low)
    sigma = theta / delta
    first = inverse * rhs * (1.0 / theta)
    early_copies = []
    for side in range(2):
        far = 4 - 4 * side
        for at, value in enumerate((rhs[far : far + 1], diag[far : far + 1])):
            out_early[side, at : at + 1, :] = value
        early_copies.append(
            pltpu.make_async_remote_copy(
                src_ref=out_early.at[side],
                dst_ref=in_early.at[1 - side],
                send_sem=early_send.at[side],
                recv_sem=early_recv.at[1 - side],
                device_id=(to[side], group),
                device_id_type=MESH,
            )
        )

        @pl.when(has[side])
        def _():
            early_copies[side].start()

    corners = corner_values(first)
    product = lex_ref[0] * spread(corners[0:1])
    for q in range(1, 8):
        product = product + lex_ref[q] * spread(corners[q : q + 1])
    nodes = gather_sums(product)
    pack_copies, far_copies = ([], [])
    for side in range(2):
        near, far = (4 * side, 4 - 4 * side)
        for at, value in enumerate((nodes[near : near + 1], nodes[far : far + 1])):
            out_pack[side, at : at + 1, :] = value
        out_far[side] = nodes[near : near + 1]
        pack_copies.append(
            pltpu.make_async_remote_copy(
                src_ref=out_pack.at[side],
                dst_ref=in_pack.at[1 - side],
                send_sem=pack_send.at[side],
                recv_sem=pack_recv.at[1 - side],
                device_id=(to[side], group),
                device_id_type=MESH,
            )
        )
        far_copies.append(
            pltpu.make_async_remote_copy(
                src_ref=out_far.at[side],
                dst_ref=in_far.at[1 - side],
                send_sem=far_send.at[side],
                recv_sem=far_recv.at[1 - side],
                device_id=(skip[side], group),
                device_id_type=MESH,
            )
        )

        @pl.when(beyond[side])
        def _():
            far_copies[side].start()

        @pl.when(has[side])
        def _():
            pack_copies[side].start()

    for side in range(2):

        @pl.when(has[side])
        def _():
            ops_copies[1 - side].wait_recv()
            early_copies[1 - side].wait_recv()
            pack_copies[1 - side].wait_recv()

        @pl.when(beyond[side])
        def _():
            far_copies[1 - side].wait_recv()

    low, high = (in_pack[0], in_pack[1])
    far_inverse = 1.0 / jnp.where(real, planes(in_early[0][1:2], in_early[1][1:2]), 1.0)
    far_rhs = planes(in_early[0][0:1], in_early[1][0:1])
    far_first = far_inverse * far_rhs * (1.0 / theta)
    far_remain = far_rhs - planes(low[1:2] + in_far[0], high[1:2] + in_far[1])
    remain = rhs - (nodes + planes(low[0:1], high[0:1]))
    rho = 1.0 / sigma
    rho_new = 1.0 / (2.0 * sigma - rho)
    second = rho_new * rho * first + 2.0 * rho_new / delta * inverse * remain
    far_second = rho_new * rho * far_first + 2.0 * rho_new / delta * far_inverse * far_remain
    rho = rho_new
    rho_new = 1.0 / (2.0 * sigma - rho)

    corners = corner_values(second)
    ends = (jnp.where(sub < 4, far_second, second), jnp.where(sub < 4, second, far_second))
    product = lex_ref[0] * spread(corners[0:1])
    for q in range(1, 8):
        product = product + lex_ref[q] * spread(corners[q : q + 1])
    for q in range(8):
        shift = q // 2 % 2 * STRIDE + q % 2
        value = ends[q // 4]
        product = product + near_ref[q] * (pltpu.roll(value, LANES - shift, 1) if shift else value)
    remain = remain - gather_sums(product)
    third = rho_new * rho * second + 2.0 * rho_new / delta * inverse * remain
    answer = first + second + third

    picked = join_parts(jnp.dot(parts_of(corner_values(answer)), own_hot, preferred_element_type=jnp.float32))
    for h in range(2):
        for a in range(4):
            value = i31_ref[0, a] * picked[0:4] + i31_ref[1, a] * picked[4:8]
            block = sum(weights[4 * h + q] * spread(value[q : q + 1]) for q in range(4))
            out_ref[8 * (2 * a + h) : 8 * (2 * a + h) + 8, :] = block

    for copy in own_copies:
        copy.wait_send()
    for side in range(2):

        @pl.when(has[side])
        def _():
            for copy in side_copies[side]:
                copy.wait_send()
            ops_copies[side].wait_send()
            pack_copies[side].wait_send()
            early_copies[side].wait_send()

        @pl.when(beyond[side])
        def _():
            far_copies[side].wait_send()


def one_layer(resid7, interp73, interp31, elem_ops, conn):
    slabs, groups = (lax.axis_size("slab"), lax.axis_size("grp"))
    dma = pltpu.SemaphoreType.DMA
    return pl.pallas_call(
        functools.partial(cycle_kernel, slabs, groups),
        out_shape=pltpu.VMEM((64, 128), jnp.float32),
        in_specs=[pl.BlockSpec(memory_space=pl.ANY)] * 3 + [SMEM] * 2,
        out_specs=VMEM,
        scratch_shapes=[
            pltpu.VMEM((8, LINE), jnp.int32),
            pltpu.VMEM((8, 8, LINE), jnp.float32),
            pltpu.VMEM((512, 128), jnp.float32),
            dma((3,)),
            pltpu.VMEM((8, 8, LANES), jnp.float32),
            pltpu.VMEM((8, 8, LANES), jnp.float32),
            pltpu.VMEM((2, 2, LANES), jnp.float32),
            pltpu.VMEM((groups - 1, 2, 2, LANES), jnp.float32),
            pltpu.VMEM((2, groups, 2, LANES), jnp.float32),
            pltpu.VMEM((2, 2, LANES), jnp.float32),
            pltpu.VMEM((2, 2, LANES), jnp.float32),
            pltpu.VMEM((2, 1, LANES), jnp.float32),
            pltpu.VMEM((2, 1, LANES), jnp.float32),
            dma((groups - 1,)),
            dma((groups - 1,)),
            dma((2, groups)),
            dma((2, groups)),
            dma((2,)),
            dma((2,)),
            dma((2,)),
            dma((2,)),
            dma((2,)),
            dma((2,)),
            pltpu.VMEM((2, 2, LANES), jnp.float32),
            pltpu.VMEM((2, 2, LANES), jnp.float32),
            dma((2,)),
            dma((2,)),
        ],
        compiler_params=pltpu.CompilerParams(collective_id=0, has_side_effects=True),
    )(conn, elem_ops, resid7, interp73.T, interp31.T)


def dispatch(resid7, interp73, interp31, elem_ops, conn, faces):
    if conn.shape[1] == LINE and resid7.shape[1] == 128 and lax.axis_size("grp") > 1:
        return one_layer(resid7, interp73, interp31, elem_ops, conn)
    return local(resid7, interp73, interp31, elem_ops, conn, faces)


def solution(mesh):
    in_specs = (
        P(None, ("slab", "grp")),
        P(),
        P(),
        P(None, None, "slab"),
        P(None, "slab"),
        P(None, "slab", None),
    )
    out_specs = P(None, ("slab", "grp"))
    return jax.shard_map(dispatch, mesh=mesh, in_specs=in_specs, out_specs=out_specs, check_vma=False)
```
